32 devices in a mesh: blk: 8 (over z, x), table: 4 (over y, core).
Axes of the slice: x: 2, y: 2, z: 4, core: 2. Of those that a mesh axis runs over, the one named last changes fastest.
Arguments:
- hot_slab: bfloat16 [128, 128], P('blk'), may hold values from -1.5 to 1.5
- hot_ids: int32 [4096, 16], P(('blk', 'table')), may hold values from 0 to 127
- dense: bfloat16 [4096, 128], P(('blk', 'table')), may hold values from -6 to 6
- cold_ids: int32 [4096, 26], P(('blk', 'table')), may hold values from 0 to 511
- table_slot: int32 [26], replicated, may hold values from 0 to 27, as said below
- cold_tables: bfloat16 [28, 512, 128], P('table'), may hold values from -6 to 6
- down_rank: bfloat16 [3456, 512], replicated, may hold values from -0.109375 to 0.109375
- up_rank: bfloat16 [512, 3456], replicated, may hold values from -0.25 to 0.25
- cross_bias: float32 [3456], replicated, may hold values from -3 to 3
- cotangent: bfloat16 [4096, 3456], P(('blk', 'table')), may hold values from -6 to 6
Outputs:
- crossed: bfloat16 [4096, 3456], P(('blk', 'table'))
- table_grad: float32 [8, 28, 512, 128], P('blk', 'table')
The draws below stay inside these ranges and needn't reach their ends.
Inputs may be any that keep to these rules, and one draw needn't show every extreme that they name: `table_slot`: distinct values; some owner has all 7 of its slots taken.
All inputs are finite; a program needn't handle non-finite values.
Results may differ from the reference program's by a relative error of at most 0.0052.
Values may be sent and summed in bfloat16 or wider, within the bound.
No kernel may reach another device: no remote copies, remote signals or barrier semaphores. Data moves between devices by JAX's collectives and lax.ppermute only.
A program may use at most 64 MiB of HBM per device.

```python
import jax
import jax.numpy as jnp
from jax import lax

D = 128
NT = 26
RANK = 512
SAMP_DEV = 128
BAG = 16
CROWS = 512
SLOTS = 7
HOT = 128
SAMPLES = 4096
FEAT = 3456
N_BLK = 8
N_TABLE = 4


def draw_table_slot(key, part):
    total = N_TABLE * SLOTS
    shuffled = jax.random.permutation(jax.random.fold_in(key, 11), total)
    full_owner = jax.random.randint(jax.random.fold_in(key, 12), (), 0, N_TABLE)
    owner_of = jnp.arange(total) // SLOTS
    score = jnp.where(owner_of == full_owner, shuffled - total, shuffled)
    order = jnp.argsort(score, stable=True)
    chosen = order[:NT]
    mixing = jax.random.permutation(jax.random.fold_in(key, 13), NT)
    return chosen[mixing].astype(jnp.int32)


def touch_ends(entries, key, least, top_value):
    index_at = [jax.random.randint(jax.random.fold_in(key, axis), (), 0, length) for axis, length in enumerate(entries.shape)]
    longest = entries.shape.index(max(entries.shape))
    beside = index_at[:longest] + [(index_at[longest] + 1) % entries.shape[longest]] + index_at[longest + 1:]
    return entries.at[tuple(index_at)].set(least).at[tuple(beside)].set(top_value)


def block_scale(rng, extent, split, least, top_value):
    def one(dim, blocks):
        heights = jax.random.uniform(jax.random.fold_in(jax.random.fold_in(rng, 6), dim), (blocks,), jnp.float32, least / len(split), top_value / len(split))
        return jnp.repeat(jnp.exp(heights), extent[dim] // blocks).reshape((-1,) + (1,) * (len(extent) - dim - 1))

    factor_of = one(*split[0])
    for cut in split[1:]:
        factor_of = factor_of * one(*cut)
    return factor_of


def bell_draw(rng, shape, scale, limit, shards=(), held_as=jnp.bfloat16):
    array = jax.random.normal(rng, shape, jnp.float32) * scale
    if len(shards) > 0:
        array = block_scale(rng, shape, shards, -0.22, 0.18) * array
    return jnp.clip(array, min=-limit, max=limit).astype(held_as)


def setup_inputs(seed: int = 0) -> dict:
    seeds = jax.random.split(jax.random.key(seed), 11)
    hot_slab = bell_draw(seeds[0], (HOT, D), 0.25, 1.5, ((0, 8),))
    hot_ids = touch_ends(jax.random.randint(seeds[1], (SAMPLES, BAG), 0, HOT), jax.random.fold_in(seeds[1], 1), 0, HOT - 1).astype(jnp.int32)
    dense = bell_draw(seeds[2], (SAMPLES, D), 1.0, 6.0, ((0, 32),))
    cold_ids = touch_ends(jax.random.randint(seeds[3], (SAMPLES, NT), 0, CROWS), jax.random.fold_in(seeds[3], 1), 0, CROWS - 1).astype(jnp.int32)
    table_slot = draw_table_slot(jax.random.fold_in(seeds[10], 71), 0)
    cold_tables = bell_draw(seeds[5], (N_TABLE * SLOTS, CROWS, D), 1.0, 6.0, ((0, 4),))
    down_rank = bell_draw(seeds[6], (FEAT, RANK), FEAT ** -0.5, 0.109375)
    up_rank = bell_draw(seeds[7], (RANK, FEAT), RANK ** -0.5, 0.25)
    cross_bias = bell_draw(seeds[8], (FEAT,), 0.5, 3.0, (), jnp.float32)
    cotangent = bell_draw(seeds[9], (SAMPLES, FEAT), 1.0, 6.0, ((0, 32),))
    return {"hot_slab": hot_slab, "hot_ids": hot_ids, "dense": dense, "cold_ids": cold_ids, "table_slot": table_slot, "cold_tables": cold_tables, "down_rank": down_rank, "up_rank": up_rank, "cross_bias": cross_bias, "cotangent": cotangent}


def reference(hot_slab, hot_ids, dense, cold_ids, table_slot, cold_tables, down_rank, up_rank, cross_bias, cotangent):
    group_rows = SAMP_DEV * N_TABLE
    slot_total = N_TABLE * SLOTS
    hot_group = hot_ids.reshape(N_BLK, group_rows, BAG)
    dense_group = dense.reshape(N_BLK, group_rows, D)
    cold_group = cold_ids.reshape(N_BLK, group_rows, NT)
    cot_group = cotangent.reshape(N_BLK, group_rows, FEAT)

    def one_group(group_args):
        ids_hot, dense_part, ids_cold, cot_part = group_args
        pooled = jnp.sum(hot_slab[ids_hot].astype(jnp.float32), axis=1)
        front_row = (dense_part.astype(jnp.float32) + pooled).astype(jnp.bfloat16)
        cold_rows = cold_tables[table_slot[None, :], ids_cold]
        features = jnp.concatenate([front_row[:, None, :], cold_rows], axis=1).reshape(group_rows, FEAT)
        low_rank = jnp.dot(features, down_rank, preferred_element_type=jnp.float32).astype(jnp.bfloat16)
        gate = jnp.dot(low_rank, up_rank, preferred_element_type=jnp.float32) + cross_bias[None, :]
        feat_wide = features.astype(jnp.float32)
        crossed = (feat_wide * gate + feat_wide).astype(jnp.bfloat16)
        cot_wide = cot_part.astype(jnp.float32)
        mixed = (cot_wide * feat_wide).astype(jnp.bfloat16)
        grad_low = jnp.dot(mixed, up_rank.T, preferred_element_type=jnp.float32).astype(jnp.bfloat16)
        grad_in = cot_wide * (gate + 1.0) + jnp.dot(grad_low, down_rank.T, preferred_element_type=jnp.float32)
        grad_in = grad_in.astype(jnp.bfloat16)
        grad_cold = grad_in.reshape(group_rows, NT + 1, D)[:, 1:, :]
        segment = (table_slot[None, :] * CROWS + ids_cold).astype(jnp.int32)
        summed = jax.ops.segment_sum(grad_cold.reshape(group_rows * NT, D).astype(jnp.float32), segment.reshape(-1), num_segments=slot_total * CROWS)
        return crossed, summed.reshape(slot_total, CROWS, D)

    crossed, table_grad = lax.map(one_group, (hot_group, dense_group, cold_group, cot_group))
    return crossed.reshape(SAMPLES, FEAT), table_grad
```

```python
import functools

import jax
import jax.numpy as jnp
from jax import lax
from jax.experimental import pallas as pl
from jax.experimental.pallas import tpu as pltpu
from jax.sharding import PartitionSpec as P

BF16 = jnp.bfloat16
F32 = jnp.float32
CHUNKS = 2
GROUP = 4
VMEM = pl.BlockSpec(memory_space=pltpu.VMEM)
SMEM = pl.BlockSpec(memory_space=pltpu.SMEM)


def peer(index, mask, count):
    return index ^ mask if count & (count - 1) == 0 else lax.rem(index + mask, count)


def peer_static(index, mask, count):
    return index ^ mask if count & (count - 1) == 0 else (index + mask) % count


def params(mib):
    return pltpu.CompilerParams(vmem_limit_bytes=mib << 20)


def invert_slots(slot_ref, inverse, tables, total):
    for slot in range(total):
        inverse[slot] = -1
    for table in range(tables):
        inverse[slot_ref[table]] = table


def lane_block(index, width):
    return pl.ds(pl.multiple_of(index * width, width), width)


def lookup_kernel(first, count, owners, slots, extra, *refs):
    slot_ref = refs[0]
    ids = refs[1 : 1 + owners]
    tables = refs[1 + owners]
    shards = refs[2 + owners : 2 + owners + extra]
    outs = refs[2 + owners + extra : 2 + 2 * owners + extra]
    inverse, lines = refs[2 + 2 * owners + extra :]
    batch = ids[0].shape[1]
    rows = tables.shape[1]
    me = lax.axis_index("table")
    invert_slots(slot_ref, inverse, ids[0].shape[0], owners * slots)
    for step in range(count):
        table = inverse[me * slots + first + step]
        for k in range(owners):
            line = ids[k][pl.ds(jnp.maximum(table, 0), 1), :]
            lines[pl.ds(k * 8 + step, 1), :] = jnp.where(table >= 0, line, -1)
    columns = lines[...].T
    position = lax.broadcasted_iota(jnp.int32, (batch, rows), 1)
    for step in range(count):
        picks = [
            jnp.where(columns[:, k * 8 + step : k * 8 + step + 1] == position, 1.0, 0.0).astype(BF16)
            for k in range(owners)
        ]
        found = jnp.dot(
            jnp.concatenate(picks, axis=0), tables[first + step], preferred_element_type=F32
        ).astype(BF16)
        for k in range(owners):
            outs[k][pl.ds(step * batch, batch), :] = found[k * batch : (k + 1) * batch]
    height = shards[0].shape[0] if extra else 0
    for r in range(extra):
        for k in range(owners):
            outs[k][pl.ds(count * batch + r * height, height), :] = shards[r][...]


def slot_list(first, count, owners):
    return [(k, first + step, step) for k in range(owners) for step in range(count)]


def table_of(inverse, me, k, slot, owners, slots):
    return inverse[peer(me, k, owners) * slots + slot]


def accumulate(items, tables, got, down, up, cot, batch, width):
    low = None
    for at in range(0, len(items), GROUP):
        group = range(at, min(at + GROUP, len(items)))
        rows = [got[items[i][0]][pl.ds(items[i][2] * batch, batch), :] for i in group]
        spots = [jnp.maximum(tables[i], 0) + 1 for i in group]
        x = jnp.concatenate(rows, axis=1)
        w_down = jnp.concatenate([down[lane_block(s, width), :] for s in spots], axis=0)
        w_up = jnp.concatenate([up[:, lane_block(s, width)] for s in spots], axis=1)
        c = jnp.concatenate([cot[:, lane_block(s, width)] for s in spots], axis=1)
        mixed = (c.astype(F32) * x.astype(F32)).astype(BF16)
        part = jnp.dot(x, w_down, preferred_element_type=F32)
        part_grad = lax.dot_general(
            mixed, w_up, (((1,), (1,)), ((), ())), preferred_element_type=F32
        )
        low, grad = (part, part_grad) if low is None else (low + part, grad + part_grad)
    return low, grad


def grads_of(items, tables, outs, low, grad_low, down, up, bias, cot, batch, width):
    for at in range(0, len(items), GROUP):
        group = range(at, min(at + GROUP, len(items)))
        spots = [jnp.maximum(tables[i], 0) + 1 for i in group]
        w_down = jnp.concatenate([down[lane_block(s, width), :] for s in spots], axis=0)
        w_up = jnp.concatenate([up[:, lane_block(s, width)] for s in spots], axis=1)
        c = jnp.concatenate([cot[:, lane_block(s, width)] for s in spots], axis=1)
        b = jnp.concatenate([bias[pl.ds(s, 1), :] for s in spots], axis=1)
        gate = jnp.dot(low, w_up, preferred_element_type=F32) + b
        back = lax.dot_general(
            grad_low, w_down, (((1,), (1,)), ((), ())), preferred_element_type=F32
        )
        out = (c.astype(F32) * (gate + 1.0) + back).astype(BF16)
        for place, i in enumerate(group):
            outs[items[i][0]][pl.ds(items[i][2] * batch, batch), :] = out[
                :, place * width : (place + 1) * width
            ]


def first_kernel(first, count, owners, slots, blocks, extra, *refs):
    slot_ref = refs[0]
    got = refs[1 : 1 + owners]
    own, hot_ids, dense, down, up, cot = refs[1 + owners : 7 + owners]
    low_out, grad_out, front_out = refs[7 + owners : 10 + owners]
    (inverse,) = refs[10 + owners :]
    batch, width = dense.shape
    height = own.shape[0]
    me = lax.axis_index("table")
    mine = lax.axis_index("blk")
    invert_slots(slot_ref, inverse, cot.shape[1] // width - 1, owners * slots)
    row = lax.broadcasted_iota(jnp.int32, (height, batch), 0)
    counts, shards = [], []
    for k in [None] + list(range(owners)):
        for r in range(extra if k is not None else 1):
            if k is None:
                base, live = mine * height, True
                shards.append(own[...])
            else:
                mask = r * owners + peer(me, k, owners) + 1
                base = jnp.where(mask < blocks, peer(mine, mask, blocks) * height, -height)
                shards.append(got[k][pl.ds(count * batch + r * height, height), :])
            total = jnp.zeros((height, batch), F32)
            for i in range(hot_ids.shape[0]):
                total += jnp.where(hot_ids[i : i + 1, :] - base == row, 1.0, 0.0)
            counts.append(total)
    counts = jnp.concatenate(counts, axis=0)
    shards = jnp.concatenate(shards, axis=0)
    pooled = lax.dot_general(
        counts.astype(BF16), shards, (((0,), (0,)), ((), ())), preferred_element_type=F32
    )
    front = (dense[...].astype(F32) + pooled).astype(BF16)
    front_out[...] = front
    items = slot_list(first, count, owners)
    tables = [table_of(inverse, me, k, slot, owners, slots) for k, slot, _ in items]
    low, grad = accumulate(items, tables, got, down, up, cot, batch, width)
    mixed = (cot[:, :width].astype(F32) * front.astype(F32)).astype(BF16)
    low += jnp.dot(front, down[:width, :], preferred_element_type=F32)
    grad += lax.dot_general(
        mixed, up[:, :width], (((1,), (1,)), ((), ())), preferred_element_type=F32
    )
    low_out[...] = low
    grad_out[...] = grad


def second_kernel(first, count, grads_first, grads_count, owners, slots, *refs):
    slot_ref = refs[0]
    got = refs[1 : 1 + owners]
    low_in, grad_in, down, up, bias, cot = refs[1 + owners : 7 + owners]
    low_out, grad_out = refs[7 + owners : 9 + owners]
    outs = refs[9 + owners : 9 + 2 * owners]
    (inverse,) = refs[9 + 2 * owners :]
    batch = cot.shape[0]
    width = bias.shape[1]
    me = lax.axis_index("table")
    invert_slots(slot_ref, inverse, cot.shape[1] // width - 1, owners * slots)
    items = slot_list(first, count, owners)
    tables = [table_of(inverse, me, k, slot, owners, slots) for k, slot, _ in items]
    low, grad = accumulate(items, tables, got, down, up, cot, batch, width)
    low = (low + low_in[...]).astype(BF16)
    grad = (grad + grad_in[...]).astype(BF16)
    low_out[...] = low
    grad_out[...] = grad
    items = slot_list(grads_first, grads_count, owners)
    tables = [table_of(inverse, me, k, slot, owners, slots) for k, slot, _ in items]
    grads_of(items, tables, outs, low, grad, down, up, bias, cot, batch, width)


def grads_kernel(first, count, owners, slots, *refs):
    slot_ref, low, grad, down, up, bias, cot = refs[:7]
    outs = refs[7 : 7 + owners]
    (inverse,) = refs[7 + owners :]
    batch = cot.shape[0]
    width = bias.shape[1]
    me = lax.axis_index("table")
    invert_slots(slot_ref, inverse, cot.shape[1] // width - 1, owners * slots)
    items = slot_list(first, count, owners)
    tables = [table_of(inverse, me, k, slot, owners, slots) for k, slot, _ in items]
    grads_of(items, tables, outs, low[...], grad[...], down, up, bias, cot, batch, width)


def crossed_kernel(spans, owners, slots, *refs):
    slot_ref = refs[0]
    chunks = len(spans)
    got = [refs[1 + c * owners : 1 + (c + 1) * owners] for c in range(chunks)]
    at = 1 + chunks * owners
    front, low_ref, up, bias = refs[at : at + 4]
    out = refs[at + 4]
    (inverse,) = refs[at + 5 :]
    batch, width = front.shape
    me = lax.axis_index("table")
    invert_slots(slot_ref, inverse, out.shape[1] // width - 1, owners * slots)
    low = low_ref[...]

    def one(x, spot):
        gate = jnp.dot(low, up[:, lane_block(spot, width)], preferred_element_type=F32)
        gate = gate + bias[pl.ds(spot, 1), :]
        x = x.astype(F32)
        out[:, lane_block(spot, width)] = (x * gate + x).astype(BF16)

    one(front[...], 0)
    for c, (first, count) in enumerate(spans):
        for k, slot, step in slot_list(first, count, owners):
            table = table_of(inverse, me, k, slot, owners, slots)

            @pl.when(table >= 0)
            def _(c=c, k=k, step=step, table=table):
                one(got[c][k][pl.ds(step * batch, batch), :], table + 1)


def scatter_kernel(first, count, owners, slots, aliased, *refs):
    slot_ref = refs[0]
    ids = refs[1 : 1 + owners]
    got = refs[1 + owners : 1 + 2 * owners]
    out, inverse, held, sems = refs[1 + 2 * owners + aliased :]
    batch = ids[0].shape[1]
    rows = out.shape[2]
    me = lax.axis_index("table")
    invert_slots(slot_ref, inverse, ids[0].shape[0], owners * slots)
    position = lax.broadcasted_iota(jnp.int32, (rows, batch), 0)
    copies = []
    for step in range(count):
        table = inverse[me * slots + first + step]
        picks, grads = [], []
        for k in range(owners):
            line = ids[k][pl.ds(jnp.maximum(table, 0), 1), :]
            line = jnp.where(table >= 0, line, -1)
            picks.append(jnp.where(position == line, 1.0, 0.0).astype(BF16))
            grads.append(got[k][pl.ds(step * batch, batch), :])
        held[step] = jnp.dot(
            jnp.concatenate(picks, axis=1),
            jnp.concatenate(grads, axis=0),
            preferred_element_type=F32,
        )
        copy = pltpu.make_async_copy(held.at[step], out.at[0, first + step], sems.at[step])
        copy.start()
        copies.append(copy)
    for copy in copies:
        copy.wait()


def on_device(
    hot_slab,
    hot_ids,
    dense,
    cold_ids,
    table_slot,
    cold_tables,
    down_rank,
    up_rank,
    cross_bias,
    cotangent,
):
    batch, width = dense.shape
    table_count = table_slot.shape[0]
    owners = lax.axis_size("table")
    blocks = lax.axis_size("blk")
    slots, table_rows = cold_tables.shape[:2]
    total = owners * slots
    rank = down_rank.shape[1]
    height = hot_slab.shape[0]
    head = -(-slots // 2)
    spans = [(0, head), (head, slots - head)] if CHUNKS == 2 and slots > 1 else None
    inverse = pltpu.SMEM((total,), jnp.int32)

    def swap(array, k):
        pairs = [(i, peer_static(i, k, owners)) for i in range(owners)]
        return lax.ppermute(array, "table", pairs)

    def exchange(arrays):
        return [arrays[0]] + [swap(arrays[k], k) for k in range(1, owners)]

    ids = cold_ids.T
    ids = [ids] + [swap(ids, k) for k in range(1, owners)]
    extra = -(-(blocks - 1) // owners)
    shards = []
    for r in range(extra):
        pairs = []
        for b in range(blocks):
            for t in range(owners):
                mask = r * owners + t + 1
                if mask < blocks:
                    pairs.append((peer_static(b, mask, blocks) * owners + t, b * owners + t))
        shards.append(lax.ppermute(hot_slab, ("blk", "table"), pairs))

    got = []
    for chunk, (first, count) in enumerate(spans):
        with_hot = extra if chunk == 0 else 0
        sends = pl.pallas_call(
            functools.partial(lookup_kernel, first, count, owners, slots, with_hot),
            out_shape=[
                jax.ShapeDtypeStruct((count * batch + with_hot * height, width), BF16)
            ]
            * owners,
            in_specs=[SMEM] + [VMEM] * (owners + 1 + with_hot),
            out_specs=[VMEM] * owners,
            scratch_shapes=[inverse, pltpu.VMEM((owners * 8, batch), jnp.int32)],
            compiler_params=params(16),
            name=f"lookup{chunk}",
        )(table_slot, *ids, cold_tables, *shards[:with_hot])
        got.append(exchange(sends))

    bias = cross_bias.reshape(-1, width)
    (first, count), (last, rest) = spans
    partial_shape = jax.ShapeDtypeStruct((batch, rank), F32)
    rank_shape = jax.ShapeDtypeStruct((batch, rank), BF16)
    low, grad, front = pl.pallas_call(
        functools.partial(first_kernel, first, count, owners, slots, blocks, extra),
        out_shape=[partial_shape, partial_shape, jax.ShapeDtypeStruct((batch, width), BF16)],
        in_specs=[SMEM] + [VMEM] * (owners + 6),
        out_specs=[VMEM] * 3,
        scratch_shapes=[inverse],
        compiler_params=params(24),
        name="first",
    )(table_slot, *got[0], hot_slab, hot_ids.T, dense, down_rank, up_rank, cotangent)
    grads_shape = [jax.ShapeDtypeStruct((n * batch, width), BF16) for n in (count, rest)]
    low, grad, *sends = pl.pallas_call(
        functools.partial(second_kernel, last, rest, first, count, owners, slots),
        out_shape=[rank_shape, rank_shape] + [grads_shape[0]] * owners,
        in_specs=[SMEM] + [VMEM] * (owners + 6),
        out_specs=[VMEM] * (2 + owners),
        scratch_shapes=[inverse],
        compiler_params=params(24),
        name="second",
    )(table_slot, *got[1], low, grad, down_rank, up_rank, bias, cotangent)
    arrived = [exchange(sends)]
    sends = pl.pallas_call(
        functools.partial(grads_kernel, last, rest, owners, slots),
        out_shape=[grads_shape[1]] * owners,
        in_specs=[SMEM] + [VMEM] * 6,
        out_specs=[VMEM] * owners,
        scratch_shapes=[inverse],
        compiler_params=params(24),
        name="grads",
    )(table_slot, low, grad, down_rank, up_rank, bias, cotangent)
    arrived.append(exchange(sends))
    crossed = pl.pallas_call(
        functools.partial(crossed_kernel, spans, owners, slots),
        out_shape=jax.ShapeDtypeStruct(cotangent.shape, BF16),
        in_specs=[SMEM] + [VMEM] * (2 * owners + 4),
        out_specs=VMEM,
        scratch_shapes=[inverse],
        compiler_params=params(24),
        name="crossed",
    )(table_slot, *got[0], *got[1], front, low, up_rank, bias)

    table_grad = None
    for chunk, (first, count) in enumerate(spans):
        more = [] if table_grad is None else [table_grad]
        table_grad = pl.pallas_call(
            functools.partial(scatter_kernel, first, count, owners, slots, len(more)),
            out_shape=jax.ShapeDtypeStruct((1, slots, table_rows, width), F32),
            in_specs=[SMEM] + [VMEM] * (2 * owners) + [pl.BlockSpec(memory_space=pl.ANY)] * len(more),
            out_specs=pl.BlockSpec(memory_space=pl.ANY),
            scratch_shapes=[
                inverse,
                pltpu.VMEM((count, table_rows, width), F32),
                pltpu.SemaphoreType.DMA((count,)),
            ],
            input_output_aliases={1 + 2 * owners: 0} if more else {},
            compiler_params=params(16),
            name=f"scatter{chunk}",
        )(table_slot, *ids, *arrived[chunk], *more)
    return crossed, table_grad


def solution(mesh):
    placed = (
        P("blk", None),
        P(("blk", "table"), None),
        P(("blk", "table"), None),
        P(("blk", "table"), None),
        P(),
        P("table", None, None),
        P(),
        P(),
        P(),
        P(("blk", "table"), None),
    )
    return jax.shard_map(
        on_device,
        mesh=mesh,
        in_specs=placed,
        out_specs=(P(("blk", "table"), None), P("blk", "table", None, None)),
        check_vma=False,
    )
```

```python
import functools

import jax
import jax.numpy as jnp
from jax import lax
from jax.experimental import pallas as pl
from jax.experimental.pallas import tpu as pltpu
from jax.sharding import PartitionSpec as P

BF16 = jnp.bfloat16
F32 = jnp.float32
ROW_PARTS = (4, 3)
GRAD_PARTS = (4, 3)
GROUP = 4
LOAD_BYTES = 9 << 20
LOAD_MIB = 1
VMEM = pl.BlockSpec(memory_space=pltpu.VMEM)
SMEM = pl.BlockSpec(memory_space=pltpu.SMEM)


def peer(index, mask, count):
    return index ^ mask if count & (count - 1) == 0 else (index + mask) % count


def params(mib):
    return pltpu.CompilerParams(vmem_limit_bytes=mib << 20)


def cut(slots, parts):
    whole = sum(parts)
    ends, total = [0], 0
    for part in parts:
        total += part
        ends.append(-(-slots * total // whole))
    return [(a, b - a) for a, b in zip(ends, ends[1:]) if b > a]


def lane_block(index, width):
    return pl.ds(pl.multiple_of(index * width, width), width)


def load_kernel(owners, slots, slot_hbm, *refs):
    count = (len(refs) - 4) // 2
    sources, results = refs[:count], refs[count : 2 * count]
    meta, slot_ref, slot_sem, sems = refs[2 * count :]
    slot_copy = pltpu.make_async_copy(slot_hbm, slot_ref, slot_sem)
    slot_copy.start()
    copies = [
        pltpu.make_async_copy(source, result, sems.at[i])
        for i, (source, result) in enumerate(zip(sources, results))
    ]
    for copy in copies:
        copy.start()
    slot_copy.wait()
    me = lax.axis_index("table")
    lane = lax.broadcasted_iota(jnp.int32, (1, meta.shape[1]), 1)
    spot = lane
    for k in range(owners):
        inside = (lane >= k * slots) & (lane < (k + 1) * slots)
        spot = jnp.where(inside, lane + ((me ^ k) - k) * slots, spot)
    table_at = jnp.full_like(lane, -1)
    place_of = jnp.zeros_like(lane)
    for table in range(slot_ref.shape[0]):
        slot = slot_ref[table]
        hit = (spot == slot) & (lane < owners * slots)
        table_at = jnp.where(hit, table, table_at)
        owner = slot // slots
        place_of = jnp.where(lane == table, slot + ((owner ^ me) - owner) * slots, place_of)
    meta[0:1, :] = table_at
    meta[1:2, :] = place_of
    for copy in copies:
        copy.wait()


def lookup_kernel(first, count, owners, slots, extra, *refs):
    meta = refs[0]
    ids = refs[1 : 1 + owners]
    tables = refs[1 + owners]
    shards = refs[2 + owners : 2 + owners + extra]
    outs = refs[2 + owners + extra : 2 + 2 * owners + extra]
    (lines,) = refs[2 + 2 * owners + extra :]
    batch = ids[0].shape[1]
    rows = tables.shape[1]
    for step in range(count):
        table = meta[0, first + step]
        for k in range(owners):
            line = ids[k][pl.ds(jnp.maximum(table, 0), 1), :]
            lines[pl.ds(k * 8 + step, 1), :] = jnp.where(table >= 0, line, -1)
    columns = lines[...].T
    position = lax.broadcasted_iota(jnp.int32, (batch, rows), 1)
    for step in range(count):
        picks = [
            jnp.where(columns[:, k * 8 + step : k * 8 + step + 1] == position, 1.0, 0.0).astype(BF16)
            for k in range(owners)
        ]
        found = jnp.dot(
            jnp.concatenate(picks, axis=0), tables[first + step], preferred_element_type=F32
        ).astype(BF16)
        for k in range(owners):
            outs[k][pl.ds(step * batch, batch), :] = found[k * batch : (k + 1) * batch]
    for shard in shards:
        height = shard.shape[0]
        for k in range(owners):
            outs[k][pl.ds(count * batch, height), :] = shard[...]


def slot_list(first, count, owners):
    return [(k, first + step, step) for k in range(owners) for step in range(count)]


def accumulate(items, tables, got, down, up, cot, batch, width):
    low = None
    for at in range(0, len(items), GROUP):
        group = range(at, min(at + GROUP, len(items)))
        rows = [got[items[i][0]][pl.ds(items[i][2] * batch, batch), :] for i in group]
        spots = [jnp.maximum(tables[i], 0) + 1 for i in group]
        x = jnp.concatenate(rows, axis=1)
        w_down = jnp.concatenate([down[lane_block(s, width), :] for s in spots], axis=0)
        w_up = jnp.concatenate([up[:, lane_block(s, width)] for s in spots], axis=1)
        c = jnp.concatenate([cot[:, lane_block(s, width)] for s in spots], axis=1)
        mixed = (c.astype(F32) * x.astype(F32)).astype(BF16)
        part = jnp.dot(x, w_down, preferred_element_type=F32)
        part_grad = lax.dot_general(
            mixed, w_up, (((1,), (1,)), ((), ())), preferred_element_type=F32
        )
        low, grad = (part, part_grad) if low is None else (low + part, grad + part_grad)
    return low, grad


def grads_of(items, tables, outs, low, grad_low, down, up, bias, cot, batch, width):
    for at in range(0, len(items), GROUP):
        group = range(at, min(at + GROUP, len(items)))
        spots = [jnp.maximum(tables[i], 0) + 1 for i in group]
        w_down = jnp.concatenate([down[lane_block(s, width), :] for s in spots], axis=0)
        w_up = jnp.concatenate([up[:, lane_block(s, width)] for s in spots], axis=1)
        c = jnp.concatenate([cot[:, lane_block(s, width)] for s in spots], axis=1)
        b = jnp.concatenate([bias[pl.ds(s, 1), :] for s in spots], axis=1)
        gate = jnp.dot(low, w_up, preferred_element_type=F32) + b
        back = lax.dot_general(
            grad_low, w_down, (((1,), (1,)), ((), ())), preferred_element_type=F32
        )
        out = (c.astype(F32) * (gate + 1.0) + back).astype(BF16)
        for place, i in enumerate(group):
            outs[items[i][0]][pl.ds(items[i][2] * batch, batch), :] = out[
                :, place * width : (place + 1) * width
            ]


def shards_kernel(offset, owners, meta, *refs):
    got, out = refs[:owners], refs[owners]
    height = out.shape[0] // owners
    for k in range(owners):
        out[k * height : (k + 1) * height, :] = got[k][offset : offset + height, :]


def first_kernel(first, count, owners, slots, *refs):
    meta = refs[0]
    got = refs[1 : 1 + owners]
    down, up, cot, low_out, grad_out = refs[1 + owners :]
    batch = cot.shape[0]
    width = got[0].shape[1]
    items = slot_list(first, count, owners)
    tables = [meta[0, k * slots + slot] for k, slot, _ in items]
    low_out[...], grad_out[...] = accumulate(items, tables, got, down, up, cot, batch, width)


def second_kernel(first, count, grads_first, grads_count, owners, slots, blocks, *refs):
    meta = refs[0]
    got = refs[1 : 1 + owners]
    held = -(-blocks // owners)
    shards = refs[1 + owners : 1 + owners + held]
    hot_ids, dense, low_in, grad_in, down, up, bias, cot = refs[1 + owners + held : 9 + owners + held]
    front_out, low_out, grad_out = refs[9 + owners + held : 12 + owners + held]
    outs = refs[12 + owners + held :]
    batch, width = dense.shape
    me = lax.axis_index("table")
    mine = lax.axis_index("blk")
    height = shards[0].shape[0] // owners
    row = lax.broadcasted_iota(jnp.int32, (height, batch), 0)
    pooled = None
    for part in range(held):
        counts = []
        for k in range(owners):
            mask = part * owners + (me ^ k)
            base = jnp.where(mask < blocks, peer(mine, mask, blocks) * height, -height)
            total = jnp.zeros((height, batch), F32)
            for i in range(hot_ids.shape[0]):
                total += jnp.where(hot_ids[i : i + 1, :] - base == row, 1.0, 0.0)
            counts.append(total)
        counts = jnp.concatenate(counts, axis=0).astype(BF16)
        more = lax.dot_general(
            counts, shards[part][...], (((0,), (0,)), ((), ())), preferred_element_type=F32
        )
        pooled = more if pooled is None else pooled + more
    front = (dense[...].astype(F32) + pooled).astype(BF16)
    front_out[...] = front
    items = slot_list(first, count, owners)
    tables = [meta[0, k * slots + slot] for k, slot, _ in items]
    low, grad = accumulate(items, tables, got, down, up, cot, batch, width)
    mixed = (cot[:, :width].astype(F32) * front.astype(F32)).astype(BF16)
    low += jnp.dot(front, down[:width, :], preferred_element_type=F32)
    grad += lax.dot_general(
        mixed, up[:, :width], (((1,), (1,)), ((), ())), preferred_element_type=F32
    )
    low = (low + low_in[...]).astype(BF16)
    grad = (grad + grad_in[...]).astype(BF16)
    low_out[...] = low
    grad_out[...] = grad
    items = slot_list(grads_first, grads_count, owners)
    tables = [meta[0, k * slots + slot] for k, slot, _ in items]
    grads_of(items, tables, outs, low, grad, down, up, bias, cot, batch, width)


def grads_kernel(first, count, owners, slots, *refs):
    meta, low, grad, down, up, bias, cot = refs[:7]
    outs = refs[7:]
    batch = cot.shape[0]
    width = bias.shape[1]
    items = slot_list(first, count, owners)
    tables = [meta[0, k * slots + slot] for k, slot, _ in items]
    grads_of(items, tables, outs, low[...], grad[...], down, up, bias, cot, batch, width)


def crossed_kernel(spans, owners, slots, *refs):
    meta = refs[0]
    chunks = len(spans)
    got = [refs[1 + c * owners : 1 + (c + 1) * owners] for c in range(chunks)]
    front, low_ref, up, bias, out, held = refs[1 + chunks * owners :]
    batch, width = front.shape
    low = low_ref[...]

    def gated(x, gate):
        x = x.astype(F32)
        return (x * gate + x).astype(BF16)

    gate = jnp.dot(low, up[:, :width], preferred_element_type=F32) + bias[0:1, :]
    out[:, :width] = gated(front[...], gate)
    for c, (first, count) in enumerate(spans):
        items = slot_list(first, count, owners)
        for at in range(0, len(items), GROUP):
            group = items[at : at + GROUP]
            spots = [jnp.maximum(meta[0, k * slots + slot], 0) + 1 for k, slot, _ in group]
            w_up = jnp.concatenate([up[:, lane_block(s, width)] for s in spots], axis=1)
            b = jnp.concatenate([bias[pl.ds(s, 1), :] for s in spots], axis=1)
            gate = jnp.dot(low, w_up, preferred_element_type=F32) + b
            for place, (k, slot, step) in enumerate(group):
                held[k * slots + slot] = gated(
                    got[c][k][pl.ds(step * batch, batch), :],
                    gate[:, place * width : (place + 1) * width],
                )
    for table in range(out.shape[1] // width - 1):
        out[:, (table + 1) * width : (table + 2) * width] = held[meta[1, table]]


def scatter_kernel(first, count, owners, slots, aliased, *refs):
    meta = refs[0]
    ids = refs[1 : 1 + owners]
    got = refs[1 + owners : 1 + 2 * owners]
    out, held, sems = refs[1 + 2 * owners + aliased :]
    batch = ids[0].shape[1]
    rows = out.shape[2]
    position = lax.broadcasted_iota(jnp.int32, (rows, batch), 0)
    copies = []
    for step in range(count):
        table = meta[0, first + step]
        picks, grads = [], []
        for k in range(owners):
            line = ids[k][pl.ds(jnp.maximum(table, 0), 1), :]
            line = jnp.where(table >= 0, line, -1)
            picks.append(jnp.where(position == line, 1.0, 0.0).astype(BF16))
            grads.append(got[k][pl.ds(step * batch, batch), :])
        held[step] = jnp.dot(
            jnp.concatenate(picks, axis=1),
            jnp.concatenate(grads, axis=0),
            preferred_element_type=F32,
        )
        copy = pltpu.make_async_copy(held.at[step], out.at[0, first + step], sems.at[step])
        copy.start()
        copies.append(copy)
    for copy in copies:
        copy.wait()


def on_device(
    hot_slab,
    hot_ids,
    dense,
    cold_ids,
    table_slot,
    cold_tables,
    down_rank,
    up_rank,
    cross_bias,
    cotangent,
):
    batch, width = dense.shape
    owners = lax.axis_size("table")
    blocks = lax.axis_size("blk")
    slots, table_rows = cold_tables.shape[:2]
    rank = down_rank.shape[1]
    height = hot_slab.shape[0]
    row_spans, grad_spans = cut(slots, ROW_PARTS), cut(slots, GRAD_PARTS)
    assert owners & (owners - 1) == 0

    def call(kernel, shapes, operands, *, mib, name, scratch=(), **more):
        return pl.pallas_call(
            kernel,
            out_shape=shapes,
            in_specs=[SMEM] + [VMEM] * (len(operands) - 1),
            out_specs=[VMEM] * len(shapes),
            scratch_shapes=list(scratch),
            compiler_params=params(mib),
            name=name,
            **more,
        )(*operands)

    def exchange(arrays):
        got = [arrays[0]]
        for k in range(1, owners):
            got.append(lax.ppermute(arrays[k], "table", [(i, i ^ k) for i in range(owners)]))
        return got

    ids = exchange([cold_ids.T] * owners)
    shard = lax.ppermute(
        hot_slab,
        ("blk", "table"),
        [
            (peer(b, t, blocks) * owners + t, b * owners + t)
            for b in range(blocks)
            for t in range(owners)
        ],
    )
    loads = [
        cold_tables,
        down_rank,
        up_rank,
        cotangent,
        cross_bias.reshape(-1, width),
        dense,
        hot_ids.T,
        cold_ids.T,
    ]
    *loads, meta = pl.pallas_call(
        functools.partial(load_kernel, owners, slots),
        out_shape=[jax.ShapeDtypeStruct(x.shape, x.dtype) for x in loads]
        + [jax.ShapeDtypeStruct((8, 128), jnp.int32)],
        in_specs=[pl.BlockSpec(memory_space=pltpu.HBM)] * (len(loads) + 1),
        out_specs=[VMEM] * (len(loads) + 1),
        scratch_shapes=[
            pltpu.SMEM(table_slot.shape, jnp.int32),
            pltpu.SemaphoreType.DMA,
            pltpu.SemaphoreType.DMA((len(loads),)),
        ],
        compiler_params=params(LOAD_MIB),
        cost_estimate=pl.CostEstimate(flops=0, transcendentals=0, bytes_accessed=LOAD_BYTES),
        name="load",
    )(*[pltpu.with_memory_space_constraint(x, pltpu.HBM) for x in [table_slot] + loads])
    tables, down, up, cot, bias, dense, hot_rows, ids[0] = loads

    got = []
    for chunk, (first, count) in enumerate(row_spans):
        tail = [shard] if chunk == 0 else []
        rows = count * batch + len(tail) * height
        sends = call(
            functools.partial(lookup_kernel, first, count, owners, slots, len(tail)),
            [jax.ShapeDtypeStruct((rows, width), BF16)] * owners,
            [meta, *ids, tables, *tail],
            scratch=[pltpu.VMEM((owners * 8, batch), jnp.int32)],
            mib=8,
            name=f"lookup{chunk}",
        )
        got.append(exchange(sends))

    (group,) = call(
        functools.partial(shards_kernel, row_spans[0][1] * batch, owners),
        [jax.ShapeDtypeStruct((owners * height, width), BF16)],
        [meta, *got[0]],
        mib=1,
        name="shards",
    )
    shards = [group]
    for mask in range(owners, blocks, owners):
        pairs = [(peer(b, mask, blocks), b) for b in range(blocks)]
        shards.append(lax.ppermute(group, "blk", pairs))

    partial_shape = jax.ShapeDtypeStruct((batch, rank), F32)
    rank_shape = jax.ShapeDtypeStruct((batch, rank), BF16)
    low, grad = call(
        functools.partial(first_kernel, *row_spans[0], owners, slots),
        [partial_shape] * 2,
        [meta, *got[0], down, up, cot],
        mib=8,
        name="first",
    )
    grad_shapes = [
        [jax.ShapeDtypeStruct((count * batch, width), BF16)] * owners for _, count in grad_spans
    ]
    front, low, grad, *sends = call(
        functools.partial(
            second_kernel, *row_spans[1], *grad_spans[0], owners, slots, blocks
        ),
        [jax.ShapeDtypeStruct((batch, width), BF16), rank_shape, rank_shape] + grad_shapes[0],
        [meta, *got[1], *shards, hot_rows, dense, low, grad, down, up, bias, cot],
        mib=8,
        name="second",
    )
    arrived = [exchange(sends)]
    for chunk in range(1, len(grad_spans)):
        sends = call(
            functools.partial(grads_kernel, *grad_spans[chunk], owners, slots),
            grad_shapes[chunk],
            [meta, low, grad, down, up, bias, cot],
            mib=8,
            name=f"grads{chunk}",
        )
        arrived.append(exchange(sends))
    (crossed,) = call(
        functools.partial(crossed_kernel, row_spans, owners, slots),
        [jax.ShapeDtypeStruct(cotangent.shape, BF16)],
        [meta, *got[0], *got[1], front, low, up, bias],
        scratch=[pltpu.VMEM((owners * slots, batch, width), BF16)],
        mib=8,
        name="crossed",
    )

    table_grad = None
    for chunk, (first, count) in enumerate(grad_spans):
        more = [] if table_grad is None else [table_grad]
        table_grad = pl.pallas_call(
            functools.partial(scatter_kernel, first, count, owners, slots, len(more)),
            out_shape=jax.ShapeDtypeStruct((1, slots, table_rows, width), F32),
            in_specs=[SMEM] + [VMEM] * (2 * owners) + [pl.BlockSpec(memory_space=pl.ANY)] * len(more),
            out_specs=pl.BlockSpec(memory_space=pl.ANY),
            scratch_shapes=[
                pltpu.VMEM((count, table_rows, width), F32),
                pltpu.SemaphoreType.DMA((count,)),
            ],
            input_output_aliases={1 + 2 * owners: 0} if more else {},
            compiler_params=params(8),
            name=f"scatter{chunk}",
        )(meta, *ids, *arrived[chunk], *more)
    return crossed, table_grad


def solution(mesh):
    placed = (
        P("blk", None),
        P(("blk", "table"), None),
        P(("blk", "table"), None),
        P(("blk", "table"), None),
        P(),
        P("table", None, None),
        P(),
        P(),
        P(),
        P(("blk", "table"), None),
    )
    return jax.shard_map(
        on_device,
        mesh=mesh,
        in_specs=placed,
        out_specs=(P(("blk", "table"), None), P("blk", "table", None, None)),
        check_vma=False,
    )
```

```python
import functools

import jax
import jax.numpy as jnp
from jax import lax
from jax.experimental import pallas as pl
from jax.experimental.pallas import tpu as pltpu
from jax.sharding import PartitionSpec as P


BF16 = jnp.bfloat16
F32 = jnp.float32
ROW_PARTS = (4, 3)
GRAD_PARTS = (4, 3)
NEAR = 2
VMEM = pl.BlockSpec(memory_space=pltpu.VMEM)
SMEM = pl.BlockSpec(memory_space=pltpu.SMEM)
HBM = pl.BlockSpec(memory_space=pltpu.HBM)
OVER_LANES = (((1,), (1,)), ((), ()))


def peer(index, mask, count):
    return index ^ mask if count & (count - 1) == 0 else (index + mask) % count


def cut(slots, parts):
    whole = sum(parts)
    ends, total = [0], 0
    for part in parts:
        total += part
        ends.append(-(-slots * total // whole))
    return [(a, b - a) for a, b in zip(ends, ends[1:])]


def load_kernel(owners, slots, slot_hbm, tables_hbm, ids_hbm, tables, ids, meta, slot_ref, sems):
    copies = [
        pltpu.make_async_copy(slot_hbm, slot_ref, sems.at[0]),
        pltpu.make_async_copy(ids_hbm, ids, sems.at[1]),
        pltpu.make_async_copy(tables_hbm, tables, sems.at[2]),
    ]
    for copy in copies:
        copy.start()
    copies[0].wait()
    me = lax.axis_index("table")
    lane = lax.broadcasted_iota(jnp.int32, (1, meta.shape[1]), 1)
    spot = lane
    for k in range(owners):
        inside = (lane >= k * slots) & (lane < (k + 1) * slots)
        spot = jnp.where(inside, lane + ((me ^ k) - k) * slots, spot)
    table_at = jnp.full_like(lane, -1)
    place_of = jnp.zeros_like(lane)
    for table in range(slot_ref.shape[0]):
        slot = slot_ref[table]
        hit = (spot == slot) & (lane < owners * slots)
        table_at = jnp.where(hit, table, table_at)
        owner = slot // slots
        place_of = jnp.where(lane == table, slot + ((owner ^ me) - owner) * slots, place_of)
    meta[0:1, :] = table_at
    meta[1:2, :] = place_of
    for copy in copies[1:]:
        copy.wait()


def find(columns, tables, masks, span, pad, outs, batch):
    first, count = span
    rows = tables.shape[1]
    position = lax.broadcasted_iota(jnp.int32, (batch, rows), 1)
    for step in range(count):
        picks = [
            jnp.where(
                columns[:, k * pad + first + step : k * pad + first + step + 1] == position, 1.0, 0.0
            ).astype(BF16)
            for k in masks
        ]
        found = jnp.dot(
            jnp.concatenate(picks, axis=0), tables[first + step], preferred_element_type=F32
        ).astype(BF16)
        for i, out in enumerate(outs):
            out[step * batch : (step + 1) * batch, :] = found[i * batch : (i + 1) * batch]


def far_first_kernel(span, owners, slots, pad, *refs):
    meta = refs[0]
    ids = refs[1 : 1 + owners]
    tables, shard, lines = refs[1 + owners : 4 + owners]
    outs = refs[4 + owners :]
    batch = ids[0].shape[1]
    height = shard.shape[0]
    for slot in range(slots):
        table = meta[0, slot]
        for k in range(owners):
            line = ids[k][pl.ds(jnp.maximum(table, 0), 1), :]
            lines[k * pad + slot : k * pad + slot + 1, :] = jnp.where(table >= 0, line, -1)
    find(lines[...].T, tables, range(NEAR, owners), span, pad, outs, batch)
    for out in outs:
        out[span[1] * batch : span[1] * batch + height, :] = shard[...]


def far_kernel(span, owners, pad, lines, tables, again, *outs):
    again[...] = lines[0:8, :]
    find(lines[...].T, tables, range(NEAR, owners), span, pad, outs, lines.shape[1])


def near_kernel(owners, slots, pad, *refs):
    (meta, lines, _, tables, shard) = refs[:5]
    down_hbm, up_hbm, cot_hbm, bias_hbm, dense_hbm, hot_hbm = refs[5:11]
    outs = refs[11 : 11 + NEAR]
    down, up, cot, bias, dense, hot = refs[11 + NEAR : 17 + NEAR]
    bias_in, sems = refs[17 + NEAR :]
    batch, width = dense.shape
    height = shard.shape[0]
    total = owners * slots
    copies = [
        pltpu.make_async_copy(bias_hbm, bias_in, sems.at[3]),
        pltpu.make_async_copy(dense_hbm, dense, sems.at[4]),
        pltpu.make_async_copy(hot_hbm, hot, sems.at[5]),
    ]
    for copy in copies:
        copy.start()
    block = lambda index: pl.ds(pl.multiple_of(index * width, width), width)
    spots = [0] + [jnp.maximum(meta[0, i], 0) + 1 for i in range(total)]
    for i, spot in enumerate(spots):
        here = pl.ds(i * width, width)
        pltpu.make_async_copy(down_hbm.at[block(spot), :], down.at[here, :], sems.at[0]).start()
        pltpu.make_async_copy(up_hbm.at[:, block(spot)], up.at[:, here], sems.at[1]).start()
        pltpu.make_async_copy(cot_hbm.at[:, block(spot)], cot.at[:, here], sems.at[2]).start()
    find(lines[...].T, tables, range(NEAR), (0, slots), pad, outs, batch)
    outs[1][slots * batch : slots * batch + height, :] = shard[...]
    for copy in copies:
        copy.wait()
    for i, spot in enumerate(spots):
        bias[i : i + 1, :] = bias_in[pl.ds(spot, 1), :]
    pltpu.make_async_copy(down, down, sems.at[0]).wait()
    pltpu.make_async_copy(up, up, sems.at[1]).wait()
    pltpu.make_async_copy(cot, cot, sems.at[2]).wait()


def shards_kernel(owners, *refs):
    shard, near = refs[:2]
    far, out = refs[2:owners], refs[owners]
    height, _ = shard.shape
    parts = [shard[...], near[near.shape[0] - height :, :]]
    parts += [ref[ref.shape[0] - height :, :] for ref in far]
    out[...] = jnp.concatenate(parts, axis=0)


def wide(ref, count, batch):
    return jnp.concatenate([ref[i * batch : (i + 1) * batch, :] for i in range(count)], axis=1)


def add_up(x, begin, down, up, cot, low, grad):
    span = slice(begin, begin + x.shape[1])
    mixed = (cot[:, span].astype(F32) * x.astype(F32)).astype(BF16)
    more = jnp.dot(x, down[span, :], preferred_element_type=F32)
    more_grad = lax.dot_general(mixed, up[:, span], OVER_LANES, preferred_element_type=F32)
    return (more, more_grad) if low is None else (low + more, grad + more_grad)


def grads_to(out, begin, count, low, grad, down, up, bias, cot):
    batch = cot.shape[0]
    width = bias.shape[1]
    span = slice(begin * width, (begin + count) * width)
    b = jnp.concatenate([bias[begin + i : begin + i + 1, :] for i in range(count)], axis=1)
    gate = jnp.dot(low, up[:, span], preferred_element_type=F32) + b
    back = lax.dot_general(grad, down[span, :], OVER_LANES, preferred_element_type=F32)
    result = (cot[:, span].astype(F32) * (gate + 1.0) + back).astype(BF16)
    for i in range(count):
        out[i * batch : (i + 1) * batch, :] = result[:, i * width : (i + 1) * width]


def first_kernel(span, owners, slots, *refs):
    near, far = refs[:NEAR], refs[NEAR:owners]
    down, up, cot, low_out, grad_out = refs[owners:]
    batch = cot.shape[0]
    width = near[0].shape[1]
    low = grad = None
    for k, ref in enumerate(near):
        x = wide(ref, slots, batch)
        low, grad = add_up(x, (1 + k * slots) * width, down, up, cot, low, grad)
    for k, ref in enumerate(far, NEAR):
        x = wide(ref, span[1], batch)
        low, grad = add_up(x, (1 + k * slots + span[0]) * width, down, up, cot, low, grad)
    low_out[...] = low
    grad_out[...] = grad


def second_kernel(span, grad_span, owners, slots, blocks, *refs):
    far = refs[: owners - NEAR]
    refs = refs[owners - NEAR :]
    held = -(-blocks // owners)
    shards = refs[:held]
    hot_ids, dense, low_in, grad_in, down, up, bias, cot = refs[held : 8 + held]
    front_out, low_out, grad_out = refs[8 + held : 11 + held]
    outs = refs[11 + held :]
    batch, width = dense.shape
    me = lax.axis_index("table")
    mine = lax.axis_index("blk")
    height = shards[0].shape[0] // owners
    row = lax.broadcasted_iota(jnp.int32, (height, batch), 0)
    pooled = None
    for part in range(held):
        counts = []
        for k in range(owners):
            mask = part * owners + (me ^ k)
            base = jnp.where(mask < blocks, peer(mine, mask, blocks) * height, -height)
            total = jnp.zeros((height, batch), F32)
            for i in range(hot_ids.shape[0]):
                total += jnp.where(hot_ids[i : i + 1, :] - base == row, 1.0, 0.0)
            counts.append(total)
        counts = jnp.concatenate(counts, axis=0).astype(BF16)
        more = lax.dot_general(
            counts, shards[part][...], (((0,), (0,)), ((), ())), preferred_element_type=F32
        )
        pooled = more if pooled is None else pooled + more
    front = (dense[...].astype(F32) + pooled).astype(BF16)
    front_out[...] = front
    low, grad = add_up(front, 0, down, up, cot, low_in[...], grad_in[...])
    for k, ref in enumerate(far, NEAR):
        x = wide(ref, span[1], batch)
        low, grad = add_up(x, (1 + k * slots + span[0]) * width, down, up, cot, low, grad)
    low = low.astype(BF16)
    grad = grad.astype(BF16)
    low_out[...] = low
    grad_out[...] = grad
    for k, out in enumerate(outs, NEAR):
        begin = 1 + k * slots + grad_span[0]
        grads_to(out, begin, grad_span[1], low, grad, down, up, bias, cot)


def grads_kernel(span, masks, slots, low, grad, down, up, bias, cot, _, *outs):
    for k, out in zip(masks, outs):
        begin = 1 + k * slots + span[0]
        grads_to(out, begin, span[1], low[...], grad[...], down, up, bias, cot)


def crossed_kernel(spans, owners, slots, *refs):
    meta = refs[0]
    chunks = len(spans)
    near = refs[1 : 1 + NEAR]
    count = owners - NEAR
    far = [refs[1 + NEAR + c * count : 1 + NEAR + (c + 1) * count] for c in range(chunks)]
    front, low, up, bias, _, out, held = refs[1 + NEAR + chunks * count :]
    batch, width = front.shape

    def gated(xs, begin):
        span = slice(begin * width, (begin + len(xs)) * width)
        gate = jnp.dot(low[...], up[:, span], preferred_element_type=F32)
        for i, x in enumerate(xs):
            part = gate[:, i * width : (i + 1) * width] + bias[begin + i : begin + i + 1, :]
            x = x.astype(F32)
            xs[i] = (x * part + x).astype(BF16)
        return xs

    out[:, :width] = gated([front[...]], 0)[0]
    runs = [(ref, k, 0, slots) for k, ref in enumerate(near)]
    runs += [(ref, k, *spans[c]) for c in range(chunks) for k, ref in enumerate(far[c], NEAR)]
    for ref, k, first, steps in runs:
        xs = [ref[i * batch : (i + 1) * batch, :] for i in range(steps)]
        for i, value in enumerate(gated(xs, 1 + k * slots + first)):
            held[k * slots + first + i] = value
    for table in range(out.shape[1] // width - 1):
        out[:, (table + 1) * width : (table + 2) * width] = held[meta[1, table]]


def summed(lines, masks, slot, grads, pad, rows):
    batch = lines.shape[1]
    position = lax.broadcasted_iota(jnp.int32, (rows, batch), 0)
    picks = [
        jnp.where(position == lines[k * pad + slot : k * pad + slot + 1, :], 1.0, 0.0).astype(BF16)
        for k in masks
    ]
    return jnp.dot(
        jnp.concatenate(picks, axis=1), jnp.concatenate(grads, axis=0), preferred_element_type=F32
    )


def scatter_kernel(span, later, owners, pad, *refs):
    lines = refs[0]
    near = refs[1 : 1 + NEAR]
    far = refs[1 + NEAR : 1 + owners]
    out, rest, held, sems = refs[1 + owners :]
    rows = out.shape[2]
    batch = lines.shape[1]
    first, count = span
    copies = []
    for step in range(count):
        slot = first + step
        grads = [ref[slot * batch : (slot + 1) * batch, :] for ref in near]
        grads += [ref[step * batch : (step + 1) * batch, :] for ref in far]
        held[step] = summed(lines, range(owners), slot, grads, pad, rows)
        copies.append(pltpu.make_async_copy(held.at[step], out.at[0, slot], sems.at[step]))
        copies[-1].start()
    for step in range(later[1]):
        slot = later[0] + step
        grads = [ref[slot * batch : (slot + 1) * batch, :] for ref in near]
        rest[step] = summed(lines, range(NEAR), slot, grads, pad, rows)
    for copy in copies:
        copy.wait()


def last_kernel(span, owners, pad, *refs):
    lines, rest = refs[:2]
    far = refs[2 : 2 + owners - NEAR]
    out, held, sems = refs[3 + owners - NEAR :]
    rows = out.shape[2]
    batch = lines.shape[1]
    copies = []
    for step in range(span[1]):
        slot = span[0] + step
        grads = [ref[step * batch : (step + 1) * batch, :] for ref in far]
        held[step] = rest[step] + summed(lines, range(NEAR, owners), slot, grads, pad, rows)
        copies.append(pltpu.make_async_copy(held.at[step], out.at[0, slot], sems.at[step]))
        copies[-1].start()
    for copy in copies:
        copy.wait()


def on_device(
    hot_slab,
    hot_ids,
    dense,
    cold_ids,
    table_slot,
    cold_tables,
    down_rank,
    up_rank,
    cross_bias,
    cotangent,
):
    batch, width = dense.shape
    owners = lax.axis_size("table")
    blocks = lax.axis_size("blk")
    slots, table_rows = cold_tables.shape[:2]
    rank = down_rank.shape[1]
    height = hot_slab.shape[0]
    total = owners * slots
    pad = -(-slots // 8) * 8
    row_spans, grad_spans = cut(slots, ROW_PARTS), cut(slots, GRAD_PARTS)
    assert owners & (owners - 1) == 0 and owners > NEAR
    far_count = owners - NEAR

    def call(kernel, shapes, operands, specs=None, *, mib, scratch=(), flops=4e9):
        return pl.pallas_call(
            kernel,
            out_shape=shapes,
            in_specs=specs or [VMEM] * len(operands),
            out_specs=[VMEM] * len(shapes),
            scratch_shapes=list(scratch),
            compiler_params=pltpu.CompilerParams(vmem_limit_bytes=mib << 20),
            cost_estimate=pl.CostEstimate(flops=int(flops), transcendentals=0, bytes_accessed=1 << 20),
        )(*operands)

    def swap(array, k):
        return lax.ppermute(array, "table", [(i, i ^ k) for i in range(owners)])

    def far_swap(arrays):
        return [swap(array, k) for k, array in enumerate(arrays, NEAR)]

    def in_hbm(array):
        return pltpu.with_memory_space_constraint(array, pltpu.HBM)

    def shape(*dims, dtype=BF16):
        return jax.ShapeDtypeStruct(dims, dtype)

    ids = cold_ids.T
    far_ids = far_swap([ids] * far_count)
    near_ids = swap(ids, 1)
    shard = lax.ppermute(
        hot_slab,
        ("blk", "table"),
        [
            (peer(b, t, blocks) * owners + t, b * owners + t)
            for b in range(blocks)
            for t in range(owners)
        ],
    )
    tables, ids, meta = call(
        functools.partial(load_kernel, owners, slots),
        [shape(*cold_tables.shape), shape(*ids.shape, dtype=jnp.int32), shape(8, 128, dtype=jnp.int32)],
        [in_hbm(table_slot), in_hbm(cold_tables), in_hbm(ids)],
        [HBM] * 3,
        scratch=[pltpu.SMEM(table_slot.shape, jnp.int32), pltpu.SemaphoreType.DMA((3,))],
        mib=1,
    )
    lines, *sends = call(
        functools.partial(far_first_kernel, row_spans[0], owners, slots, pad),
        [shape(owners * pad, batch, dtype=jnp.int32)]
        + [shape(row_spans[0][1] * batch + height, width)] * far_count,
        [meta, ids, near_ids, *far_ids, tables, shard],
        [SMEM] + [VMEM] * (owners + 2),
        mib=4,
    )
    far = [far_swap(sends)]
    again, *sends = call(
        functools.partial(far_kernel, row_spans[1], owners, pad),
        [shape(8, batch, dtype=jnp.int32)] + [shape(row_spans[1][1] * batch, width)] * far_count,
        [lines, tables],
        mib=4,
    )
    far.append(far_swap(sends))
    features = (total + 1) * width
    *near, down, up, cot, bias, dense, hot_rows = call(
        functools.partial(near_kernel, owners, slots, pad),
        [shape(slots * batch, width), shape(slots * batch + height, width)]
        + [
            shape(features, rank),
            shape(rank, features),
            shape(batch, features),
            shape(-(-(total + 1) // 8) * 8, width, dtype=F32),
            shape(batch, width),
            shape(hot_ids.shape[1], batch, dtype=jnp.int32),
        ],
        [meta, lines, again, tables, shard]
        + [
            in_hbm(x)
            for x in (
                down_rank,
                up_rank,
                cotangent,
                cross_bias.reshape(-1, width),
                dense,
                hot_ids.T,
            )
        ],
        [SMEM] + [VMEM] * 4 + [HBM] * 6,
        scratch=[
            pltpu.VMEM((cross_bias.shape[0] // width, width), F32),
            pltpu.SemaphoreType.DMA((6,)),
        ],
        mib=6,
    )
    near[1] = swap(near[1], 1)

    (group,) = call(
        functools.partial(shards_kernel, owners),
        [shape(owners * height, width)],
        [shard, near[1], *far[0]],
        mib=1,
    )
    shards = [group]
    for mask in range(owners, blocks, owners):
        pairs = [(peer(b, mask, blocks), b) for b in range(blocks)]
        shards.append(lax.ppermute(group, "blk", pairs))

    low, grad = call(
        functools.partial(first_kernel, row_spans[0], owners, slots),
        [shape(batch, rank, dtype=F32)] * 2,
        [*near, *far[0], down, up, cot],
        mib=6,
    )
    front, low, grad, *sends = call(
        functools.partial(second_kernel, row_spans[1], grad_spans[0], owners, slots, blocks),
        [shape(batch, width), shape(batch, rank), shape(batch, rank)]
        + [shape(grad_spans[0][1] * batch, width)] * far_count,
        [*far[1], *shards, hot_rows, dense, low, grad, down, up, bias, cot],
        mib=6,
    )
    far_grads = [far_swap(sends)]
    sends = call(
        functools.partial(grads_kernel, grad_spans[1], range(NEAR, owners), slots),
        [shape(grad_spans[1][1] * batch, width)] * far_count,
        [low, grad, down, up, bias, cot, front],
        mib=6,
    )
    far_grads.append(far_swap(sends))
    near_grads = call(
        functools.partial(grads_kernel, (0, slots), range(NEAR), slots),
        [shape(slots * batch, width)] * NEAR,
        [low, grad, down, up, bias, cot, sends[0]],
        mib=6,
    )
    last_near = near_grads[0]
    near_grads = [near_grads[0], swap(near_grads[1], 1)]
    (crossed,) = call(
        functools.partial(crossed_kernel, row_spans, owners, slots),
        [shape(*cotangent.shape)],
        [meta, *near, *far[0], *far[1], front, low, up, bias, last_near],
        [SMEM] + [VMEM] * (NEAR + 2 * far_count + 5),
        scratch=[pltpu.VMEM((total, batch, width), BF16)],
        mib=6,
    )

    (first, count), later = grad_spans
    grads_shape = shape(1, slots, table_rows, width, dtype=F32)
    table_grad, rest = pl.pallas_call(
        functools.partial(scatter_kernel, grad_spans[0], later, owners, pad),
        out_shape=[grads_shape, shape(later[1], table_rows, width, dtype=F32)],
        in_specs=[VMEM] * (1 + owners),
        out_specs=[pl.BlockSpec(memory_space=pl.ANY), VMEM],
        scratch_shapes=[
            pltpu.VMEM((count, table_rows, width), F32),
            pltpu.SemaphoreType.DMA((count,)),
        ],
        compiler_params=pltpu.CompilerParams(vmem_limit_bytes=6 << 20),
        name="scatter",
    )(lines, *near_grads, *far_grads[0])
    table_grad = pl.pallas_call(
        functools.partial(last_kernel, later, owners, pad),
        out_shape=grads_shape,
        in_specs=[VMEM] * (2 + far_count) + [pl.BlockSpec(memory_space=pl.ANY)],
        out_specs=pl.BlockSpec(memory_space=pl.ANY),
        scratch_shapes=[
            pltpu.VMEM((later[1], table_rows, width), F32),
            pltpu.SemaphoreType.DMA((later[1],)),
        ],
        input_output_aliases={2 + far_count: 0},
        compiler_params=pltpu.CompilerParams(vmem_limit_bytes=6 << 20),
        name="last",
    )(lines, rest, *far_grads[1], table_grad)
    return crossed, table_grad


def solution(mesh):
    placed = (
        P("blk", None),
        P(("blk", "table"), None),
        P(("blk", "table"), None),
        P(("blk", "table"), None),
        P(),
        P("table", None, None),
        P(),
        P(),
        P(),
        P(("blk", "table"), None),
    )

    return jax.shard_map(
        on_device,
        mesh=mesh,
        in_specs=placed,
        out_specs=(P(("blk", "table"), None), P("blk", "table", None, None)),
        check_vma=False,
    )
```

```python
import functools

import jax
import jax.numpy as jnp
from jax import lax
from jax.experimental import pallas as pl
from jax.experimental.pallas import tpu as pltpu
from jax.sharding import PartitionSpec as P


BF16 = jnp.bfloat16
F32 = jnp.float32
ROW_PARTS = (3, 4)
GRAD_PARTS = (4, 3)
NEAR = 2
VMEM = pl.BlockSpec(memory_space=pltpu.VMEM)
SMEM = pl.BlockSpec(memory_space=pltpu.SMEM)
HBM = pl.BlockSpec(memory_space=pltpu.HBM)
OVER_LANES = (((1,), (1,)), ((), ()))


def peer(index, mask, count):
    return index ^ mask if count & (count - 1) == 0 else (index + mask) % count


def cut(slots, parts):
    whole = sum(parts)
    ends, total = [0], 0
    for part in parts:
        total += part
        ends.append(-(-slots * total // whole))
    return [(a, b - a) for a, b in zip(ends, ends[1:])]


def load_kernel(owners, slots, slot_hbm, tables_hbm, ids_hbm, tables, ids, meta, slot_ref, sems):
    copies = [
        pltpu.make_async_copy(slot_hbm, slot_ref, sems.at[0]),
        pltpu.make_async_copy(ids_hbm, ids, sems.at[1]),
        pltpu.make_async_copy(tables_hbm, tables, sems.at[2]),
    ]
    for copy in copies:
        copy.start()
    copies[0].wait()
    me = lax.axis_index("table")
    lane = lax.broadcasted_iota(jnp.int32, (1, meta.shape[1]), 1)
    spot = lane
    for k in range(owners):
        inside = (lane >= k * slots) & (lane < (k + 1) * slots)
        spot = jnp.where(inside, lane + ((me ^ k) - k) * slots, spot)
    table_at = jnp.full_like(lane, -1)
    place_of = jnp.zeros_like(lane)
    for table in range(slot_ref.shape[0]):
        slot = slot_ref[table]
        hit = (spot == slot) & (lane < owners * slots)
        table_at = jnp.where(hit, table, table_at)
        owner = slot // slots
        place_of = jnp.where(lane == table, slot + ((owner ^ me) - owner) * slots, place_of)
    meta[0:1, :] = table_at
    meta[1:2, :] = place_of
    for copy in copies[1:]:
        copy.wait()


def find(columns, tables, masks, span, pad, outs, batch):
    first, count = span
    rows = tables.shape[1]
    position = lax.broadcasted_iota(jnp.int32, (batch, rows), 1)
    for step in range(count):
        picks = [
            jnp.where(
                columns[:, k * pad + first + step : k * pad + first + step + 1] == position, 1.0, 0.0
            ).astype(BF16)
            for k in masks
        ]
        found = jnp.dot(
            jnp.concatenate(picks, axis=0), tables[first + step], preferred_element_type=F32
        ).astype(BF16)
        for i, out in enumerate(outs):
            out[step * batch : (step + 1) * batch, :] = found[i * batch : (i + 1) * batch]


def far_first_kernel(span, owners, slots, pad, *refs):
    meta = refs[0]
    ids = refs[1 : 1 + owners]
    tables, shard, lines = refs[1 + owners : 4 + owners]
    outs = refs[4 + owners :]
    batch = ids[0].shape[1]
    height = shard.shape[0]
    for slot in range(slots):
        table = meta[0, slot]
        for k in range(owners):
            line = ids[k][pl.ds(jnp.maximum(table, 0), 1), :]
            lines[k * pad + slot : k * pad + slot + 1, :] = jnp.where(table >= 0, line, -1)
    find(lines[...].T, tables, range(NEAR, owners), span, pad, outs, batch)
    for out in outs:
        out[span[1] * batch : span[1] * batch + height, :] = shard[...]


def far_kernel(span, owners, pad, lines, tables, again, *outs):
    again[...] = lines[0:8, :]
    find(lines[...].T, tables, range(NEAR, owners), span, pad, outs, lines.shape[1])


def partner_kernel(slots, pad, lines, _, tables, shard, out):
    batch = lines.shape[1]
    find(lines[...].T, tables, [1], (0, slots), pad, [out], batch)
    out[slots * batch : slots * batch + shard.shape[0], :] = shard[...]


def near_kernel(owners, slots, pad, *refs):
    meta, lines, _, tables, down_in, up_in, cot_in, bias_in = refs[:8]
    out, down, up, cot, bias = refs[8:]
    batch = lines.shape[1]
    width = bias.shape[1]
    for i in range(owners * slots + 1):
        spot = jnp.maximum(meta[0, i - 1], 0) + 1 if i else 0
        block = pl.ds(pl.multiple_of(spot * width, width), width) if i else slice(0, width)
        here = slice(i * width, (i + 1) * width)
        down[here, :] = down_in[block, :]
        up[:, here] = up_in[:, block]
        cot[:, here] = cot_in[:, block]
        bias[i : i + 1, :] = bias_in[pl.ds(spot, 1), :]
    find(lines[...].T, tables, [0], (0, slots), pad, [out], batch)


def shards_kernel(owners, *refs):
    shard, near = refs[:2]
    far, out = refs[2:owners], refs[owners]
    height, _ = shard.shape
    parts = [shard[...], near[near.shape[0] - height :, :]]
    parts += [ref[ref.shape[0] - height :, :] for ref in far]
    out[...] = jnp.concatenate(parts, axis=0)


def wide(ref, count, batch):
    return jnp.concatenate([ref[i * batch : (i + 1) * batch, :] for i in range(count)], axis=1)


def add_up(x, begin, down, up, cot, low, grad):
    span = slice(begin, begin + x.shape[1])
    mixed = (cot[:, span].astype(F32) * x.astype(F32)).astype(BF16)
    more = jnp.dot(x, down[span, :], preferred_element_type=F32)
    more_grad = lax.dot_general(mixed, up[:, span], OVER_LANES, preferred_element_type=F32)
    return (more, more_grad) if low is None else (low + more, grad + more_grad)


def grads_to(out, begin, count, low, grad, down, up, bias, cot):
    batch = cot.shape[0]
    width = bias.shape[1]
    span = slice(begin * width, (begin + count) * width)
    b = jnp.concatenate([bias[begin + i : begin + i + 1, :] for i in range(count)], axis=1)
    gate = jnp.dot(low, up[:, span], preferred_element_type=F32) + b
    back = lax.dot_general(grad, down[span, :], OVER_LANES, preferred_element_type=F32)
    result = (cot[:, span].astype(F32) * (gate + 1.0) + back).astype(BF16)
    for i in range(count):
        out[i * batch : (i + 1) * batch, :] = result[:, i * width : (i + 1) * width]


def sums_kernel(span, masks, slots, *refs):
    rows, refs = refs[: len(masks)], refs[len(masks) :]
    down, up, cot = refs[:3]
    low, grad = (ref[...] for ref in refs[3:5]) if len(refs) == 7 else (None, None)
    low_out, grad_out = refs[-2:]
    batch = cot.shape[0]
    width = rows[0].shape[1]
    for k, ref in zip(masks, rows):
        x = wide(ref, span[1], batch)
        low, grad = add_up(x, (1 + k * slots + span[0]) * width, down, up, cot, low, grad)
    low_out[...] = low
    grad_out[...] = grad


def second_kernel(span, grad_span, owners, slots, blocks, *refs):
    far = refs[: owners - NEAR]
    refs = refs[owners - NEAR :]
    held = -(-blocks // owners)
    shards = refs[:held]
    hot_ids, dense, low_in, grad_in, down, up, bias, cot = refs[held : 8 + held]
    front_out, low_out, grad_out = refs[8 + held : 11 + held]
    outs = refs[11 + held :]
    batch, width = dense.shape
    me = lax.axis_index("table")
    mine = lax.axis_index("blk")
    height = shards[0].shape[0] // owners
    row = lax.broadcasted_iota(jnp.int32, (height, batch), 0)
    pooled = None
    for part in range(held):
        counts = []
        for k in range(owners):
            mask = part * owners + (me ^ k)
            base = jnp.where(mask < blocks, peer(mine, mask, blocks) * height, -height)
            total = jnp.zeros((height, batch), F32)
            for i in range(hot_ids.shape[0]):
                total += jnp.where(hot_ids[i : i + 1, :] - base == row, 1.0, 0.0)
            counts.append(total)
        counts = jnp.concatenate(counts, axis=0).astype(BF16)
        more = lax.dot_general(
            counts, shards[part][...], (((0,), (0,)), ((), ())), preferred_element_type=F32
        )
        pooled = more if pooled is None else pooled + more
    front = (dense[...].astype(F32) + pooled).astype(BF16)
    front_out[...] = front
    low, grad = add_up(front, 0, down, up, cot, low_in[...], grad_in[...])
    for k, ref in enumerate(far, NEAR):
        x = wide(ref, span[1], batch)
        low, grad = add_up(x, (1 + k * slots + span[0]) * width, down, up, cot, low, grad)
    low = low.astype(BF16)
    grad = grad.astype(BF16)
    low_out[...] = low
    grad_out[...] = grad
    for k, out in enumerate(outs, NEAR):
        begin = 1 + k * slots + grad_span[0]
        grads_to(out, begin, grad_span[1], low, grad, down, up, bias, cot)


def grads_kernel(span, masks, slots, low, grad, down, up, bias, cot, _, *outs):
    for k, out in zip(masks, outs):
        begin = 1 + k * slots + span[0]
        grads_to(out, begin, span[1], low[...], grad[...], down, up, bias, cot)


def crossed_kernel(spans, owners, slots, *refs):
    meta = refs[0]
    chunks = len(spans)
    near = refs[1 : 1 + NEAR]
    count = owners - NEAR
    far = [refs[1 + NEAR + c * count : 1 + NEAR + (c + 1) * count] for c in range(chunks)]
    front, low, up, bias, _, out, held = refs[1 + NEAR + chunks * count :]
    batch, width = front.shape

    def gated(xs, begin):
        span = slice(begin * width, (begin + len(xs)) * width)
        gate = jnp.dot(low[...], up[:, span], preferred_element_type=F32)
        for i, x in enumerate(xs):
            part = gate[:, i * width : (i + 1) * width] + bias[begin + i : begin + i + 1, :]
            x = x.astype(F32)
            xs[i] = (x * part + x).astype(BF16)
        return xs

    out[:, :width] = gated([front[...]], 0)[0]
    runs = [(ref, k, 0, slots) for k, ref in enumerate(near)]
    runs += [(ref, k, *spans[c]) for c in range(chunks) for k, ref in enumerate(far[c], NEAR)]
    for ref, k, first, steps in runs:
        xs = [ref[i * batch : (i + 1) * batch, :] for i in range(steps)]
        for i, value in enumerate(gated(xs, 1 + k * slots + first)):
            held[k * slots + first + i] = value
    for table in range(out.shape[1] // width - 1):
        out[:, (table + 1) * width : (table + 2) * width] = held[meta[1, table]]


def summed(lines, masks, slot, grads, pad, rows):
    batch = lines.shape[1]
    position = lax.broadcasted_iota(jnp.int32, (rows, batch), 0)
    picks = [
        jnp.where(position == lines[k * pad + slot : k * pad + slot + 1, :], 1.0, 0.0).astype(BF16)
        for k in masks
    ]
    return jnp.dot(
        jnp.concatenate(picks, axis=1), jnp.concatenate(grads, axis=0), preferred_element_type=F32
    )


def scatter_kernel(span, later, owners, pad, *refs):
    lines = refs[0]
    near = refs[1 : 1 + NEAR]
    far = refs[1 + NEAR : 1 + owners]
    out, rest, held, sems = refs[1 + owners :]
    rows = out.shape[2]
    batch = lines.shape[1]
    first, count = span
    copies = []
    for step in range(count):
        slot = first + step
        grads = [ref[slot * batch : (slot + 1) * batch, :] for ref in near]
        grads += [ref[step * batch : (step + 1) * batch, :] for ref in far]
        held[step] = summed(lines, range(owners), slot, grads, pad, rows)
        copies.append(pltpu.make_async_copy(held.at[step], out.at[0, slot], sems.at[step]))
        copies[-1].start()
    for step in range(later[1]):
        slot = later[0] + step
        grads = [ref[slot * batch : (slot + 1) * batch, :] for ref in near]
        rest[step] = summed(lines, range(NEAR), slot, grads, pad, rows)
    for copy in copies:
        copy.wait()


def last_kernel(span, owners, pad, *refs):
    lines, rest = refs[:2]
    far = refs[2 : 2 + owners - NEAR]
    out, held, sems = refs[3 + owners - NEAR :]
    rows = out.shape[2]
    batch = lines.shape[1]
    copies = []
    for step in range(span[1]):
        slot = span[0] + step
        grads = [ref[step * batch : (step + 1) * batch, :] for ref in far]
        held[step] = rest[step] + summed(lines, range(NEAR, owners), slot, grads, pad, rows)
        copies.append(pltpu.make_async_copy(held.at[step], out.at[0, slot], sems.at[step]))
        copies[-1].start()
    for copy in copies:
        copy.wait()


def on_device(
    hot_slab,
    hot_ids,
    dense,
    cold_ids,
    table_slot,
    cold_tables,
    down_rank,
    up_rank,
    cross_bias,
    cotangent,
):
    batch, width = dense.shape
    owners = lax.axis_size("table")
    blocks = lax.axis_size("blk")
    slots, table_rows = cold_tables.shape[:2]
    rank = down_rank.shape[1]
    height = hot_slab.shape[0]
    total = owners * slots
    pad = -(-slots // 8) * 8
    row_spans, grad_spans = cut(slots, ROW_PARTS), cut(slots, GRAD_PARTS)
    assert owners & (owners - 1) == 0 and owners > NEAR
    far_count = owners - NEAR

    def call(kernel, shapes, operands, specs=None, *, mib, scratch=(), flops=4e9):
        return pl.pallas_call(
            kernel,
            out_shape=shapes,
            in_specs=specs or [VMEM] * len(operands),
            out_specs=[VMEM] * len(shapes),
            scratch_shapes=list(scratch),
            compiler_params=pltpu.CompilerParams(vmem_limit_bytes=mib << 20),
            cost_estimate=pl.CostEstimate(flops=int(flops), transcendentals=0, bytes_accessed=1 << 20),
        )(*operands)

    def swap(array, k):
        return lax.ppermute(array, "table", [(i, i ^ k) for i in range(owners)])

    def far_swap(arrays):
        return [swap(array, k) for k, array in enumerate(arrays, NEAR)]

    def in_hbm(array):
        return pltpu.with_memory_space_constraint(array, pltpu.HBM)

    def shape(*dims, dtype=BF16):
        return jax.ShapeDtypeStruct(dims, dtype)

    ids = cold_ids.T
    far_ids = far_swap([ids] * far_count)
    near_ids = swap(ids, 1)
    shard = lax.ppermute(
        hot_slab,
        ("blk", "table"),
        [
            (peer(b, t, blocks) * owners + t, b * owners + t)
            for b in range(blocks)
            for t in range(owners)
        ],
    )
    tables, ids, meta = call(
        functools.partial(load_kernel, owners, slots),
        [shape(*cold_tables.shape), shape(*ids.shape, dtype=jnp.int32), shape(8, 128, dtype=jnp.int32)],
        [in_hbm(table_slot), in_hbm(cold_tables), in_hbm(ids)],
        [HBM] * 3,
        scratch=[pltpu.SMEM(table_slot.shape, jnp.int32), pltpu.SemaphoreType.DMA((3,))],
        mib=1,
        flops=1e9,
    )
    lines, *sends = call(
        functools.partial(far_first_kernel, row_spans[0], owners, slots, pad),
        [shape(owners * pad, batch, dtype=jnp.int32)]
        + [shape(row_spans[0][1] * batch + height, width)] * far_count,
        [meta, ids, near_ids, *far_ids, tables, shard],
        [SMEM] + [VMEM] * (owners + 2),
        mib=4,
        flops=1e9,
    )
    far = [far_swap(sends)]
    again, *sends = call(
        functools.partial(far_kernel, row_spans[1], owners, pad),
        [shape(8, batch, dtype=jnp.int32)] + [shape(row_spans[1][1] * batch, width)] * far_count,
        [lines, tables],
        mib=4,
        flops=5e8,
    )
    far.append(far_swap(sends))
    features = (total + 1) * width
    (partner,) = call(
        functools.partial(partner_kernel, slots, pad),
        [shape(slots * batch + height, width)],
        [lines, again, tables, shard],
        mib=4,
        flops=5e8,
    )
    mine, down, up, cot, bias = call(
        functools.partial(near_kernel, owners, slots, pad),
        [
            shape(slots * batch, width),
            shape(features, rank),
            shape(rank, features),
            shape(batch, features),
            shape(-(-(total + 1) // 8) * 8, width, dtype=F32),
        ],
        [meta, lines, partner, tables]
        + [down_rank, up_rank, cotangent, cross_bias.reshape(-1, width)],
        [SMEM] + [VMEM] * 7,
        mib=6,
    )
    hot_rows = hot_ids.T
    near = [mine, swap(partner, 1)]

    (group,) = call(
        functools.partial(shards_kernel, owners),
        [shape(owners * height, width)],
        [shard, near[1], *far[0]],
        mib=1,
    )
    shards = [group]
    for mask in range(owners, blocks, owners):
        pairs = [(peer(b, mask, blocks), b) for b in range(blocks)]
        shards.append(lax.ppermute(group, "blk", pairs))

    sums = [shape(batch, rank, dtype=F32)] * 2
    low, grad = call(
        functools.partial(sums_kernel, (0, slots), range(NEAR), slots),
        sums,
        [*near, down, up, cot],
        mib=6,
    )
    low, grad = call(
        functools.partial(sums_kernel, row_spans[0], range(NEAR, owners), slots),
        sums,
        [*far[0], down, up, cot, low, grad],
        mib=6,
    )
    front, low, grad, *sends = call(
        functools.partial(second_kernel, row_spans[1], grad_spans[0], owners, slots, blocks),
        [shape(batch, width), shape(batch, rank), shape(batch, rank)]
        + [shape(grad_spans[0][1] * batch, width)] * far_count,
        [*far[1], *shards, hot_rows, dense, low, grad, down, up, bias, cot],
        mib=6,
    )
    far_grads = [far_swap(sends)]
    sends = call(
        functools.partial(grads_kernel, grad_spans[1], range(NEAR, owners), slots),
        [shape(grad_spans[1][1] * batch, width)] * far_count,
        [low, grad, down, up, bias, cot, front],
        mib=6,
    )
    far_grads.append(far_swap(sends))
    near_grads = call(
        functools.partial(grads_kernel, (0, slots), range(NEAR), slots),
        [shape(slots * batch, width)] * NEAR,
        [low, grad, down, up, bias, cot, sends[0]],
        mib=6,
    )
    last_near = near_grads[0]
    near_grads = [near_grads[0], swap(near_grads[1], 1)]
    (crossed,) = call(
        functools.partial(crossed_kernel, row_spans, owners, slots),
        [shape(*cotangent.shape)],
        [meta, *near, *far[0], *far[1], front, low, up, bias, last_near],
        [SMEM] + [VMEM] * (NEAR + 2 * far_count + 5),
        scratch=[pltpu.VMEM((total, batch, width), BF16)],
        mib=6,
    )

    (first, count), later = grad_spans
    grads_shape = shape(1, slots, table_rows, width, dtype=F32)
    table_grad, rest = pl.pallas_call(
        functools.partial(scatter_kernel, grad_spans[0], later, owners, pad),
        out_shape=[grads_shape, shape(later[1], table_rows, width, dtype=F32)],
        in_specs=[VMEM] * (1 + owners),
        out_specs=[pl.BlockSpec(memory_space=pl.ANY), VMEM],
        scratch_shapes=[
            pltpu.VMEM((count, table_rows, width), F32),
            pltpu.SemaphoreType.DMA((count,)),
        ],
        compiler_params=pltpu.CompilerParams(vmem_limit_bytes=6 << 20),
        name="scatter",
    )(lines, *near_grads, *far_grads[0])
    table_grad = pl.pallas_call(
        functools.partial(last_kernel, later, owners, pad),
        out_shape=grads_shape,
        in_specs=[VMEM] * (2 + far_count) + [pl.BlockSpec(memory_space=pl.ANY)],
        out_specs=pl.BlockSpec(memory_space=pl.ANY),
        scratch_shapes=[
            pltpu.VMEM((later[1], table_rows, width), F32),
            pltpu.SemaphoreType.DMA((later[1],)),
        ],
        input_output_aliases={2 + far_count: 0},
        compiler_params=pltpu.CompilerParams(vmem_limit_bytes=6 << 20),
        name="last",
    )(lines, rest, *far_grads[1], table_grad)
    return crossed, table_grad


def solution(mesh):
    placed = (
        P("blk", None),
        P(("blk", "table"), None),
        P(("blk", "table"), None),
        P(("blk", "table"), None),
        P(),
        P("table", None, None),
        P(),
        P(),
        P(),
        P(("blk", "table"), None),
    )

    return jax.shard_map(
        on_device,
        mesh=mesh,
        in_specs=placed,
        out_specs=(P(("blk", "table"), None), P("blk", "table", None, None)),
        check_vma=False,
    )
```

```python
import functools

import jax
import jax.numpy as jnp
from jax import lax
from jax.experimental import pallas as pl
from jax.experimental.pallas import tpu as pltpu
from jax.sharding import PartitionSpec as P


BF16 = jnp.bfloat16
F32 = jnp.float32
ROW_PARTS = (3, 4)
GRAD_PARTS = (4, 3)
NEAR = 2
VMEM = pl.BlockSpec(memory_space=pltpu.VMEM)
SMEM = pl.BlockSpec(memory_space=pltpu.SMEM)
HBM = pl.BlockSpec(memory_space=pltpu.HBM)
OVER_LANES = (((1,), (1,)), ((), ()))


def peer(index, mask, count):
    return index ^ mask if count & (count - 1) == 0 else (index + mask) % count


def cut(slots, parts):
    whole = sum(parts)
    ends, total = [0], 0
    for part in parts:
        total += part
        ends.append(-(-slots * total // whole))
    return [(a, b - a) for a, b in zip(ends, ends[1:])]


def cover_kernel(out):
    out[...] = jnp.zeros_like(out)


def find(columns, tables, masks, span, pad, outs, batch):
    first, count = span
    rows = tables.shape[1]
    position = lax.broadcasted_iota(jnp.int32, (batch, rows), 1)
    for step in range(count):
        picks = [
            jnp.where(
                columns[:, k * pad + first + step : k * pad + first + step + 1] == position, 1.0, 0.0
            ).astype(BF16)
            for k in masks
        ]
        found = jnp.dot(
            jnp.concatenate(picks, axis=0), tables[first + step], preferred_element_type=F32
        ).astype(BF16)
        for i, out in enumerate(outs):
            out[step * batch : (step + 1) * batch, :] = found[i * batch : (i + 1) * batch]


def far_first_kernel(span, owners, slots, pad, *refs):
    slot_ref = refs[0]
    ids = refs[2 : 2 + owners]
    tables, lines, meta = refs[2 + owners : 5 + owners]
    outs, spots = refs[5 + owners : -1], refs[-1]
    batch = ids[0].shape[1]
    for slot in range(slots):
        spots[slot] = -1
    me = lax.axis_index("table")
    lane = lax.broadcasted_iota(jnp.int32, (1, meta.shape[1]), 1)
    table_at = jnp.full_like(lane, -1)
    place_of = jnp.zeros_like(lane)
    for table in range(slot_ref.shape[0]):
        slot = slot_ref[table]
        owner = slot // slots
        place = slot + ((owner ^ me) - owner) * slots
        spots[jnp.minimum(place, slots)] = table
        table_at = jnp.where(lane == place, table, table_at)
        place_of = jnp.where(lane == table, place, place_of)
    meta[0:1, :] = table_at
    meta[1:2, :] = place_of
    for slot in range(slots):
        table = spots[slot]
        for k in range(owners):
            line = ids[k][pl.ds(jnp.maximum(table, 0), 1), :]
            lines[k * pad + slot : k * pad + slot + 1, :] = jnp.where(table >= 0, line, -1)
    find(lines[...].T, tables, range(NEAR, owners), span, pad, outs, batch)


def tail_kernel(*refs):
    count = len(refs) // 2
    for out in refs[count + 1 :]:
        height = refs[0].shape[0]
        out[out.shape[0] - height :, :] = refs[0][...]


def far_kernel(span, owners, pad, lines, tables, again, *outs):
    again[...] = lines[0:8, :]
    find(lines[...].T, tables, range(NEAR, owners), span, pad, outs, lines.shape[1])


def partner_kernel(slots, pad, lines, _, tables, shard, out):
    batch = lines.shape[1]
    find(lines[...].T, tables, [1], (0, slots), pad, [out], batch)
    out[slots * batch : slots * batch + shard.shape[0], :] = shard[...]


def near_kernel(owners, slots, pad, *refs):
    meta, lines, _, tables, down_in, up_in, cot_in, bias_in = refs[:8]
    out, down, up, cot, bias = refs[8:]
    batch = lines.shape[1]
    width = bias.shape[1]
    for i in range(owners * slots + 1):
        spot = jnp.maximum(meta[0, i - 1], 0) + 1 if i else 0
        block = pl.ds(pl.multiple_of(spot * width, width), width) if i else slice(0, width)
        here = slice(i * width, (i + 1) * width)
        down[here, :] = down_in[block, :]
        up[:, here] = up_in[:, block]
        cot[:, here] = cot_in[:, block]
        bias[i : i + 1, :] = bias_in[pl.ds(spot, 1), :]
    find(lines[...].T, tables, [0], (0, slots), pad, [out], batch)


def shards_kernel(owners, *refs):
    shard, near = refs[:2]
    far, out = refs[2:owners], refs[owners]
    height, _ = shard.shape
    parts = [shard[...], near[near.shape[0] - height :, :]]
    parts += [ref[ref.shape[0] - height :, :] for ref in far]
    out[...] = jnp.concatenate(parts, axis=0)


def wide(ref, count, batch):
    return jnp.concatenate([ref[i * batch : (i + 1) * batch, :] for i in range(count)], axis=1)


def add_up(x, begin, down, up, cot, low, grad):
    span = slice(begin, begin + x.shape[1])
    mixed = (cot[:, span].astype(F32) * x.astype(F32)).astype(BF16)
    more = jnp.dot(x, down[span, :], preferred_element_type=F32)
    more_grad = lax.dot_general(mixed, up[:, span], OVER_LANES, preferred_element_type=F32)
    return (more, more_grad) if low is None else (low + more, grad + more_grad)


def grads_to(out, begin, count, low, grad, down, up, bias, cot):
    batch = cot.shape[0]
    width = bias.shape[1]
    span = slice(begin * width, (begin + count) * width)
    b = jnp.concatenate([bias[begin + i : begin + i + 1, :] for i in range(count)], axis=1)
    gate = jnp.dot(low, up[:, span], preferred_element_type=F32) + b
    back = lax.dot_general(grad, down[span, :], OVER_LANES, preferred_element_type=F32)
    result = (cot[:, span].astype(F32) * (gate + 1.0) + back).astype(BF16)
    for i in range(count):
        out[i * batch : (i + 1) * batch, :] = result[:, i * width : (i + 1) * width]


def sums_kernel(span, masks, slots, *refs):
    rows, refs = refs[: len(masks)], refs[len(masks) :]
    down, up, cot = refs[:3]
    low, grad = (ref[...] for ref in refs[3:5]) if len(refs) == 7 else (None, None)
    low_out, grad_out = refs[-2:]
    batch = cot.shape[0]
    width = rows[0].shape[1]
    for k, ref in zip(masks, rows):
        x = wide(ref, span[1], batch)
        low, grad = add_up(x, (1 + k * slots + span[0]) * width, down, up, cot, low, grad)
    low_out[...] = low
    grad_out[...] = grad


def second_kernel(span, grad_span, owners, slots, blocks, *refs):
    far = refs[: owners - NEAR]
    refs = refs[owners - NEAR :]
    held = -(-blocks // owners)
    shards = refs[:held]
    hot_ids, dense, low_in, grad_in, down, up, bias, cot = refs[held : 8 + held]
    front_out, low_out, grad_out = refs[8 + held : 11 + held]
    outs = refs[11 + held :]
    batch, width = dense.shape
    me = lax.axis_index("table")
    mine = lax.axis_index("blk")
    height = shards[0].shape[0] // owners
    row = lax.broadcasted_iota(jnp.int32, (height, batch), 0)
    pooled = None
    for part in range(held):
        counts = []
        for k in range(owners):
            mask = part * owners + (me ^ k)
            base = jnp.where(mask < blocks, peer(mine, mask, blocks) * height, -height)
            total = jnp.zeros((height, batch), F32)
            for i in range(hot_ids.shape[0]):
                total += jnp.where(hot_ids[i : i + 1, :] - base == row, 1.0, 0.0)
            counts.append(total)
        counts = jnp.concatenate(counts, axis=0).astype(BF16)
        more = lax.dot_general(
            counts, shards[part][...], (((0,), (0,)), ((), ())), preferred_element_type=F32
        )
        pooled = more if pooled is None else pooled + more
    front = (dense[...].astype(F32) + pooled).astype(BF16)
    front_out[...] = front
    low, grad = add_up(front, 0, down, up, cot, low_in[...], grad_in[...])
    for k, ref in enumerate(far, NEAR):
        x = wide(ref, span[1], batch)
        low, grad = add_up(x, (1 + k * slots + span[0]) * width, down, up, cot, low, grad)
    low = low.astype(BF16)
    grad = grad.astype(BF16)
    low_out[...] = low
    grad_out[...] = grad
    for k, out in enumerate(outs, NEAR):
        begin = 1 + k * slots + grad_span[0]
        grads_to(out, begin, grad_span[1], low, grad, down, up, bias, cot)


def grads_kernel(span, masks, slots, low, grad, down, up, bias, cot, _, *outs):
    for k, out in zip(masks, outs):
        begin = 1 + k * slots + span[0]
        grads_to(out, begin, span[1], low[...], grad[...], down, up, bias, cot)


def crossed_kernel(spans, owners, slots, *refs):
    meta = refs[0]
    chunks = len(spans)
    near = refs[1 : 1 + NEAR]
    count = owners - NEAR
    far = [refs[1 + NEAR + c * count : 1 + NEAR + (c + 1) * count] for c in range(chunks)]
    front, low, up, bias, _, out, held = refs[1 + NEAR + chunks * count :]
    batch, width = front.shape

    def gated(xs, begin):
        span = slice(begin * width, (begin + len(xs)) * width)
        gate = jnp.dot(low[...], up[:, span], preferred_element_type=F32)
        for i, x in enumerate(xs):
            part = gate[:, i * width : (i + 1) * width] + bias[begin + i : begin + i + 1, :]
            x = x.astype(F32)
            xs[i] = (x * part + x).astype(BF16)
        return xs

    out[:, :width] = gated([front[...]], 0)[0]
    runs = [(ref, k, 0, slots) for k, ref in enumerate(near)]
    runs += [(ref, k, *spans[c]) for c in range(chunks) for k, ref in enumerate(far[c], NEAR)]
    for ref, k, first, steps in runs:
        xs = [ref[i * batch : (i + 1) * batch, :] for i in range(steps)]
        for i, value in enumerate(gated(xs, 1 + k * slots + first)):
            held[k * slots + first + i] = value
    for table in range(out.shape[1] // width - 1):
        out[:, (table + 1) * width : (table + 2) * width] = held[meta[1, table]]


def summed(lines, masks, slot, grads, pad, rows):
    batch = lines.shape[1]
    position = lax.broadcasted_iota(jnp.int32, (rows, batch), 0)
    picks = [
        jnp.where(position == lines[k * pad + slot : k * pad + slot + 1, :], 1.0, 0.0).astype(BF16)
        for k in masks
    ]
    return jnp.dot(
        jnp.concatenate(picks, axis=1), jnp.concatenate(grads, axis=0), preferred_element_type=F32
    )


def scatter_kernel(span, later, owners, pad, *refs):
    lines = refs[0]
    near = refs[1 : 1 + NEAR]
    far = refs[1 + NEAR : 1 + owners]
    out, rest, held, sems = refs[1 + owners :]
    rows = out.shape[2]
    batch = lines.shape[1]
    first, count = span
    copies = []
    for step in range(count):
        slot = first + step
        grads = [ref[slot * batch : (slot + 1) * batch, :] for ref in near]
        grads += [ref[step * batch : (step + 1) * batch, :] for ref in far]
        held[step] = summed(lines, range(owners), slot, grads, pad, rows)
        copies.append(pltpu.make_async_copy(held.at[step], out.at[0, slot], sems.at[step]))
        copies[-1].start()
    for step in range(later[1]):
        slot = later[0] + step
        grads = [ref[slot * batch : (slot + 1) * batch, :] for ref in near]
        rest[step] = summed(lines, range(NEAR), slot, grads, pad, rows)
    for copy in copies:
        copy.wait()


def last_kernel(span, owners, pad, *refs):
    lines, rest = refs[:2]
    far = refs[2 : 2 + owners - NEAR]
    out, held, sems = refs[3 + owners - NEAR :]
    rows = out.shape[2]
    batch = lines.shape[1]
    copies = []
    for step in range(span[1]):
        slot = span[0] + step
        grads = [ref[step * batch : (step + 1) * batch, :] for ref in far]
        held[step] = rest[step] + summed(lines, range(NEAR, owners), slot, grads, pad, rows)
        copies.append(pltpu.make_async_copy(held.at[step], out.at[0, slot], sems.at[step]))
        copies[-1].start()
    for copy in copies:
        copy.wait()


def on_device(
    hot_slab,
    hot_ids,
    dense,
    cold_ids,
    table_slot,
    cold_tables,
    down_rank,
    up_rank,
    cross_bias,
    cotangent,
):
    batch, width = dense.shape
    owners = lax.axis_size("table")
    blocks = lax.axis_size("blk")
    slots, table_rows = cold_tables.shape[:2]
    rank = down_rank.shape[1]
    height = hot_slab.shape[0]
    total = owners * slots
    pad = -(-slots // 8) * 8
    row_spans, grad_spans = cut(slots, ROW_PARTS), cut(slots, GRAD_PARTS)
    assert owners & (owners - 1) == 0 and owners > NEAR
    far_count = owners - NEAR

    def call(kernel, shapes, operands, specs=None, *, mib, scratch=(), aliases=None, flops=4e9):
        return pl.pallas_call(
            kernel,
            out_shape=shapes,
            in_specs=[VMEM] * len(operands) if specs is None else specs,
            out_specs=[VMEM] * len(shapes),
            scratch_shapes=list(scratch),
            input_output_aliases=aliases or {},
            compiler_params=pltpu.CompilerParams(vmem_limit_bytes=mib << 20),
            cost_estimate=pl.CostEstimate(flops=int(flops), transcendentals=0, bytes_accessed=1 << 20),
        )(*operands)

    def swap(array, k):
        return lax.ppermute(array, "table", [(i, i ^ k) for i in range(owners)])

    def far_swap(arrays):
        return [swap(array, k) for k, array in enumerate(arrays, NEAR)]

    def shape(*dims, dtype=BF16):
        return jax.ShapeDtypeStruct(dims, dtype)

    ids = cold_ids.T
    far_ids = far_swap([ids] * far_count)
    near_ids = swap(ids, 1)
    shard = lax.ppermute(
        hot_slab,
        ("blk", "table"),
        [
            (peer(b, t, blocks) * owners + t, b * owners + t)
            for b in range(blocks)
            for t in range(owners)
        ],
    )
    (cover,) = call(cover_kernel, [shape(8, 128, dtype=jnp.int32)], [], mib=1)
    tables = cold_tables
    lines, meta, *sends = call(
        functools.partial(far_first_kernel, row_spans[0], owners, slots, pad),
        [shape(owners * pad, batch, dtype=jnp.int32), shape(8, 128, dtype=jnp.int32)]
        + [shape(row_spans[0][1] * batch + height, width)] * far_count,
        [table_slot, cover, ids, near_ids, *far_ids, tables],
        [SMEM] + [VMEM] * (owners + 2),
        scratch=[pltpu.SMEM((slots + 1,), jnp.int32)],
        mib=4,
        flops=1e9,
    )
    sends = call(
        tail_kernel,
        [shape(*array.shape) for array in sends],
        [shard, *sends],
        aliases={1 + i: i for i in range(far_count)},
        mib=1,
        flops=1e8,
    )
    far = [far_swap(sends)]
    again, *sends = call(
        functools.partial(far_kernel, row_spans[1], owners, pad),
        [shape(8, batch, dtype=jnp.int32)] + [shape(row_spans[1][1] * batch, width)] * far_count,
        [lines, tables],
        mib=4,
        flops=5e8,
    )
    far.append(far_swap(sends))
    features = (total + 1) * width
    (partner,) = call(
        functools.partial(partner_kernel, slots, pad),
        [shape(slots * batch + height, width)],
        [lines, again, tables, shard],
        mib=4,
        flops=5e8,
    )
    mine, down, up, cot, bias = call(
        functools.partial(near_kernel, owners, slots, pad),
        [
            shape(slots * batch, width),
            shape(features, rank),
            shape(rank, features),
            shape(batch, features),
            shape(-(-(total + 1) // 8) * 8, width, dtype=F32),
        ],
        [meta, lines, partner, tables]
        + [down_rank, up_rank, cotangent, cross_bias.reshape(-1, width)],
        [SMEM] + [VMEM] * 7,
        mib=6,
    )
    hot_rows = hot_ids.T
    near = [mine, swap(partner, 1)]

    (group,) = call(
        functools.partial(shards_kernel, owners),
        [shape(owners * height, width)],
        [shard, near[1], *far[0]],
        mib=1,
    )
    shards = [group]
    for mask in range(owners, blocks, owners):
        pairs = [(peer(b, mask, blocks), b) for b in range(blocks)]
        shards.append(lax.ppermute(group, "blk", pairs))

    sums = [shape(batch, rank, dtype=F32)] * 2
    low, grad = call(
        functools.partial(sums_kernel, (0, slots), range(NEAR), slots),
        sums,
        [*near, down, up, cot],
        mib=6,
    )
    low, grad = call(
        functools.partial(sums_kernel, row_spans[0], range(NEAR, owners), slots),
        sums,
        [*far[0], down, up, cot, low, grad],
        mib=6,
    )
    front, low, grad, *sends = call(
        functools.partial(second_kernel, row_spans[1], grad_spans[0], owners, slots, blocks),
        [shape(batch, width), shape(batch, rank), shape(batch, rank)]
        + [shape(grad_spans[0][1] * batch, width)] * far_count,
        [*far[1], *shards, hot_rows, dense, low, grad, down, up, bias, cot],
        mib=6,
    )
    far_grads = [far_swap(sends)]
    sends = call(
        functools.partial(grads_kernel, grad_spans[1], range(NEAR, owners), slots),
        [shape(grad_spans[1][1] * batch, width)] * far_count,
        [low, grad, down, up, bias, cot, front],
        mib=6,
    )
    far_grads.append(far_swap(sends))
    near_grads = call(
        functools.partial(grads_kernel, (0, slots), range(NEAR), slots),
        [shape(slots * batch, width)] * NEAR,
        [low, grad, down, up, bias, cot, sends[0]],
        mib=6,
    )
    last_near = near_grads[0]
    near_grads = [near_grads[0], swap(near_grads[1], 1)]
    (crossed,) = call(
        functools.partial(crossed_kernel, row_spans, owners, slots),
        [shape(*cotangent.shape)],
        [meta, *near, *far[0], *far[1], front, low, up, bias, last_near],
        [SMEM] + [VMEM] * (NEAR + 2 * far_count + 5),
        scratch=[pltpu.VMEM((total, batch, width), BF16)],
        mib=6,
    )

    (first, count), later = grad_spans
    grads_shape = shape(1, slots, table_rows, width, dtype=F32)
    table_grad, rest = pl.pallas_call(
        functools.partial(scatter_kernel, grad_spans[0], later, owners, pad),
        out_shape=[grads_shape, shape(later[1], table_rows, width, dtype=F32)],
        in_specs=[VMEM] * (1 + owners),
        out_specs=[pl.BlockSpec(memory_space=pl.ANY), VMEM],
        scratch_shapes=[
            pltpu.VMEM((count, table_rows, width), F32),
            pltpu.SemaphoreType.DMA((count,)),
        ],
        compiler_params=pltpu.CompilerParams(vmem_limit_bytes=6 << 20),
        name="scatter",
    )(lines, *near_grads, *far_grads[0])
    table_grad = pl.pallas_call(
        functools.partial(last_kernel, later, owners, pad),
        out_shape=grads_shape,
        in_specs=[VMEM] * (2 + far_count) + [pl.BlockSpec(memory_space=pl.ANY)],
        out_specs=pl.BlockSpec(memory_space=pl.ANY),
        scratch_shapes=[
            pltpu.VMEM((later[1], table_rows, width), F32),
            pltpu.SemaphoreType.DMA((later[1],)),
        ],
        input_output_aliases={2 + far_count: 0},
        compiler_params=pltpu.CompilerParams(vmem_limit_bytes=6 << 20),
        name="last",
    )(lines, rest, *far_grads[1], table_grad)
    return crossed, table_grad


def solution(mesh):
    placed = (
        P("blk", None),
        P(("blk", "table"), None),
        P(("blk", "table"), None),
        P(("blk", "table"), None),
        P(),
        P("table", None, None),
        P(),
        P(),
        P(),
        P(("blk", "table"), None),
    )

    return jax.shard_map(
        on_device,
        mesh=mesh,
        in_specs=placed,
        out_specs=(P(("blk", "table"), None), P("blk", "table", None, None)),
        check_vma=False,
    )
```

```python
import functools

import jax
import jax.numpy as jnp
from jax import lax
from jax.experimental import pallas as pl
from jax.experimental.pallas import tpu as pltpu
from jax.sharding import PartitionSpec as P


BF16 = jnp.bfloat16
F32 = jnp.float32
ROW_PARTS = (3, 4)
GRAD_PARTS = (4, 3)
NEAR = 2
VMEM = pl.BlockSpec(memory_space=pltpu.VMEM)
SMEM = pl.BlockSpec(memory_space=pltpu.SMEM)
HBM = pl.BlockSpec(memory_space=pltpu.HBM)
OVER_LANES = (((1,), (1,)), ((), ()))


def peer(index, mask, count):
    return index ^ mask if count & (count - 1) == 0 else (index + mask) % count


def cut(slots, parts):
    whole = sum(parts)
    ends, total = [0], 0
    for part in parts:
        total += part
        ends.append(-(-slots * total // whole))
    return [(a, b - a) for a, b in zip(ends, ends[1:])]


def cover_kernel(out):
    out[...] = jnp.zeros_like(out)


def find(columns, tables, masks, span, pad, outs, batch):
    first, count = span
    rows = tables.shape[1]
    position = lax.broadcasted_iota(jnp.int32, (batch, rows), 1)
    for step in range(count):
        picks = [
            jnp.where(
                columns[:, k * pad + first + step : k * pad + first + step + 1] == position, 1.0, 0.0
            ).astype(BF16)
            for k in masks
        ]
        found = jnp.dot(
            jnp.concatenate(picks, axis=0), tables[first + step], preferred_element_type=F32
        ).astype(BF16)
        for i, out in enumerate(outs):
            out[step * batch : (step + 1) * batch, :] = found[i * batch : (i + 1) * batch]


def far_first_kernel(span, owners, slots, pad, *refs):
    slot_ref = refs[0]
    ids = refs[2 : 2 + owners]
    tables, lines, meta = refs[2 + owners : 5 + owners]
    outs, spots = refs[5 + owners : -1], refs[-1]
    batch = ids[0].shape[1]
    for slot in range(slots):
        spots[slot] = -1
    me = lax.axis_index("table")
    lane = lax.broadcasted_iota(jnp.int32, (1, meta.shape[1]), 1)
    table_at = jnp.full_like(lane, -1)
    place_of = jnp.zeros_like(lane)
    for table in range(slot_ref.shape[0]):
        slot = slot_ref[table]
        owner = slot // slots
        place = slot + ((owner ^ me) - owner) * slots
        spots[jnp.minimum(place, slots)] = table
        table_at = jnp.where(lane == place, table, table_at)
        place_of = jnp.where(lane == table, place, place_of)
    meta[0:1, :] = table_at
    meta[1:2, :] = place_of
    for slot in range(slots):
        table = spots[slot]
        for k in range(owners):
            line = ids[k][pl.ds(jnp.maximum(table, 0), 1), :]
            lines[k * pad + slot : k * pad + slot + 1, :] = jnp.where(table >= 0, line, -1)
    find(lines[...].T, tables, range(NEAR, owners), span, pad, outs, batch)


def tail_kernel(*refs):
    count = len(refs) // 2
    for out in refs[count + 1 :]:
        height = refs[0].shape[0]
        out[out.shape[0] - height :, :] = refs[0][...]


def far_kernel(span, owners, pad, lines, tables, again, *outs):
    again[...] = lines[0:8, :]
    find(lines[...].T, tables, range(NEAR, owners), span, pad, outs, lines.shape[1])


def partner_kernel(slots, pad, lines, _, tables, shard, out):
    batch = lines.shape[1]
    find(lines[...].T, tables, [1], (0, slots), pad, [out], batch)
    out[slots * batch : slots * batch + shard.shape[0], :] = shard[...]


def near_kernel(owners, slots, pad, *refs):
    meta, lines, _, tables, down_in, up_in, cot_in, bias_in = refs[:8]
    out, down, up, cot, bias = refs[8:]
    batch = lines.shape[1]
    width = bias.shape[1]
    for i in range(owners * slots + 1):
        spot = jnp.maximum(meta[0, i - 1], 0) + 1 if i else 0
        block = pl.ds(pl.multiple_of(spot * width, width), width) if i else slice(0, width)
        here = slice(i * width, (i + 1) * width)
        down[here, :] = down_in[block, :]
        up[:, here] = up_in[:, block]
        cot[:, here] = cot_in[:, block]
        bias[i : i + 1, :] = bias_in[pl.ds(spot, 1), :]
    find(lines[...].T, tables, [0], (0, slots), pad, [out], batch)


def shards_kernel(owners, *refs):
    shard, near = refs[:2]
    far, out = refs[2:owners], refs[owners]
    height, _ = shard.shape
    parts = [shard[...], near[near.shape[0] - height :, :]]
    parts += [ref[ref.shape[0] - height :, :] for ref in far]
    out[...] = jnp.concatenate(parts, axis=0)


def wide(ref, count, batch):
    return jnp.concatenate([ref[i * batch : (i + 1) * batch, :] for i in range(count)], axis=1)


def add_up(x, begin, down, up, cot, low, grad):
    span = slice(begin, begin + x.shape[1])
    mixed = (cot[:, span].astype(F32) * x.astype(F32)).astype(BF16)
    more = jnp.dot(x, down[span, :], preferred_element_type=F32)
    more_grad = lax.dot_general(mixed, up[:, span], OVER_LANES, preferred_element_type=F32)
    return (more, more_grad) if low is None else (low + more, grad + more_grad)


def grads_to(out, begin, count, low, grad, down, up, bias, cot):
    batch = cot.shape[0]
    width = bias.shape[1]
    span = slice(begin * width, (begin + count) * width)
    b = jnp.concatenate([bias[begin + i : begin + i + 1, :] for i in range(count)], axis=1)
    gate = jnp.dot(low, up[:, span], preferred_element_type=F32) + b
    back = lax.dot_general(grad, down[span, :], OVER_LANES, preferred_element_type=F32)
    result = (cot[:, span].astype(F32) * (gate + 1.0) + back).astype(BF16)
    for i in range(count):
        out[i * batch : (i + 1) * batch, :] = result[:, i * width : (i + 1) * width]


def sums_kernel(span, masks, slots, *refs):
    rows, refs = refs[: len(masks)], refs[len(masks) :]
    down, up, cot = refs[:3]
    low, grad = (ref[...] for ref in refs[3:5]) if len(refs) == 7 else (None, None)
    low_out, grad_out = refs[-2:]
    batch = cot.shape[0]
    width = rows[0].shape[1]
    for k, ref in zip(masks, rows):
        x = wide(ref, span[1], batch)
        low, grad = add_up(x, (1 + k * slots + span[0]) * width, down, up, cot, low, grad)
    low_out[...] = low
    grad_out[...] = grad


def counts_kernel(owners, blocks, group, hot_ids, dense, counts, base):
    batch = dense.shape[0]
    me = lax.axis_index("table")
    mine = lax.axis_index("blk")
    height = group.shape[0] // owners
    row = lax.broadcasted_iota(jnp.int32, (height, batch), 0)
    for part in range(-(-blocks // owners)):
        for k in range(owners):
            mask = part * owners + (me ^ k)
            first = jnp.where(mask < blocks, peer(mine, mask, blocks) * height, -height)
            total = jnp.zeros((height, batch), F32)
            for i in range(hot_ids.shape[0]):
                total += jnp.where(hot_ids[i : i + 1, :] - first == row, 1.0, 0.0)
            begin = (part * owners + k) * height
            counts[begin : begin + height, :] = total.astype(BF16)
    pooled = lax.dot_general(
        counts[: owners * height, :],
        group[...],
        (((0,), (0,)), ((), ())),
        preferred_element_type=F32,
    )
    base[...] = dense[...].astype(F32) + pooled


def second_kernel(span, grad_span, owners, slots, blocks, *refs):
    far = refs[: owners - NEAR]
    refs = refs[owners - NEAR :]
    held = -(-blocks // owners)
    shards = refs[:held]
    counts, base, low_in, grad_in, down, up, bias, cot = refs[held : 8 + held]
    front_out, low_out, grad_out = refs[8 + held : 11 + held]
    outs = refs[11 + held :]
    batch, width = base.shape
    pooled = base[...]
    for part in range(1, held):
        rows = counts[part * shards[part].shape[0] : (part + 1) * shards[part].shape[0], :]
        pooled += lax.dot_general(
            rows, shards[part][...], (((0,), (0,)), ((), ())), preferred_element_type=F32
        )
    front = pooled.astype(BF16)
    front_out[...] = front
    low, grad = add_up(front, 0, down, up, cot, low_in[...], grad_in[...])
    for k, ref in enumerate(far, NEAR):
        x = wide(ref, span[1], batch)
        low, grad = add_up(x, (1 + k * slots + span[0]) * width, down, up, cot, low, grad)
    low = low.astype(BF16)
    grad = grad.astype(BF16)
    low_out[...] = low
    grad_out[...] = grad
    for k, out in enumerate(outs, NEAR):
        begin = 1 + k * slots + grad_span[0]
        grads_to(out, begin, grad_span[1], low, grad, down, up, bias, cot)


def grads_kernel(span, masks, slots, low, grad, down, up, bias, cot, _, *outs):
    for k, out in zip(masks, outs):
        begin = 1 + k * slots + span[0]
        grads_to(out, begin, span[1], low[...], grad[...], down, up, bias, cot)


def crossed_kernel(spans, owners, slots, *refs):
    meta = refs[0]
    chunks = len(spans)
    near = refs[1 : 1 + NEAR]
    count = owners - NEAR
    far = [refs[1 + NEAR + c * count : 1 + NEAR + (c + 1) * count] for c in range(chunks)]
    front, low, up, bias, _, out, held = refs[1 + NEAR + chunks * count :]
    batch, width = front.shape

    def gated(xs, begin):
        span = slice(begin * width, (begin + len(xs)) * width)
        gate = jnp.dot(low[...], up[:, span], preferred_element_type=F32)
        for i, x in enumerate(xs):
            part = gate[:, i * width : (i + 1) * width] + bias[begin + i : begin + i + 1, :]
            x = x.astype(F32)
            xs[i] = (x * part + x).astype(BF16)
        return xs

    out[:, :width] = gated([front[...]], 0)[0]
    runs = [(ref, k, 0, slots) for k, ref in enumerate(near)]
    runs += [(ref, k, *spans[c]) for c in range(chunks) for k, ref in enumerate(far[c], NEAR)]
    for ref, k, first, steps in runs:
        xs = [ref[i * batch : (i + 1) * batch, :] for i in range(steps)]
        for i, value in enumerate(gated(xs, 1 + k * slots + first)):
            held[k * slots + first + i] = value
    for table in range(out.shape[1] // width - 1):
        out[:, (table + 1) * width : (table + 2) * width] = held[meta[1, table]]


def summed(lines, masks, slot, grads, pad, rows):
    batch = lines.shape[1]
    position = lax.broadcasted_iota(jnp.int32, (rows, batch), 0)
    picks = [
        jnp.where(position == lines[k * pad + slot : k * pad + slot + 1, :], 1.0, 0.0).astype(BF16)
        for k in masks
    ]
    return jnp.dot(
        jnp.concatenate(picks, axis=1), jnp.concatenate(grads, axis=0), preferred_element_type=F32
    )


def scatter_kernel(span, later, owners, pad, *refs):
    lines = refs[0]
    near = refs[1 : 1 + NEAR]
    far = refs[1 + NEAR : 1 + owners]
    out, rest, held, sems = refs[1 + owners :]
    rows = out.shape[2]
    batch = lines.shape[1]
    first, count = span
    copies = []
    for step in range(count):
        slot = first + step
        grads = [ref[slot * batch : (slot + 1) * batch, :] for ref in near]
        grads += [ref[step * batch : (step + 1) * batch, :] for ref in far]
        held[step] = summed(lines, range(owners), slot, grads, pad, rows)
        copies.append(pltpu.make_async_copy(held.at[step], out.at[0, slot], sems.at[step]))
        copies[-1].start()
    for step in range(later[1]):
        slot = later[0] + step
        grads = [ref[slot * batch : (slot + 1) * batch, :] for ref in near]
        rest[step] = summed(lines, range(NEAR), slot, grads, pad, rows)
    for copy in copies:
        copy.wait()


def last_kernel(span, owners, pad, *refs):
    lines, rest = refs[:2]
    far = refs[2 : 2 + owners - NEAR]
    out, held, sems = refs[3 + owners - NEAR :]
    rows = out.shape[2]
    batch = lines.shape[1]
    copies = []
    for step in range(span[1]):
        slot = span[0] + step
        grads = [ref[step * batch : (step + 1) * batch, :] for ref in far]
        held[step] = rest[step] + summed(lines, range(NEAR, owners), slot, grads, pad, rows)
        copies.append(pltpu.make_async_copy(held.at[step], out.at[0, slot], sems.at[step]))
        copies[-1].start()
    for copy in copies:
        copy.wait()


def on_device(
    hot_slab,
    hot_ids,
    dense,
    cold_ids,
    table_slot,
    cold_tables,
    down_rank,
    up_rank,
    cross_bias,
    cotangent,
):
    batch, width = dense.shape
    owners = lax.axis_size("table")
    blocks = lax.axis_size("blk")
    slots, table_rows = cold_tables.shape[:2]
    rank = down_rank.shape[1]
    height = hot_slab.shape[0]
    total = owners * slots
    pad = -(-slots // 8) * 8
    row_spans, grad_spans = cut(slots, ROW_PARTS), cut(slots, GRAD_PARTS)
    assert owners & (owners - 1) == 0 and owners > NEAR
    far_count = owners - NEAR

    def call(kernel, shapes, operands, specs=None, *, mib, scratch=(), aliases=None, flops=4e9):
        return pl.pallas_call(
            kernel,
            out_shape=shapes,
            in_specs=[VMEM] * len(operands) if specs is None else specs,
            out_specs=[VMEM] * len(shapes),
            scratch_shapes=list(scratch),
            input_output_aliases=aliases or {},
            compiler_params=pltpu.CompilerParams(vmem_limit_bytes=mib << 20),
            cost_estimate=pl.CostEstimate(flops=int(flops), transcendentals=0, bytes_accessed=1 << 20),
        )(*operands)

    def swap(array, k):
        return lax.ppermute(array, "table", [(i, i ^ k) for i in range(owners)])

    def far_swap(arrays):
        return [swap(array, k) for k, array in enumerate(arrays, NEAR)]

    def shape(*dims, dtype=BF16):
        return jax.ShapeDtypeStruct(dims, dtype)

    ids = cold_ids.T
    far_ids = far_swap([ids] * far_count)
    near_ids = swap(ids, 1)
    shard = lax.ppermute(
        hot_slab,
        ("blk", "table"),
        [
            (peer(b, t, blocks) * owners + t, b * owners + t)
            for b in range(blocks)
            for t in range(owners)
        ],
    )
    (cover,) = call(cover_kernel, [shape(8, 128, dtype=jnp.int32)], [], mib=1)
    tables = cold_tables
    lines, meta, *sends = call(
        functools.partial(far_first_kernel, row_spans[0], owners, slots, pad),
        [shape(owners * pad, batch, dtype=jnp.int32), shape(8, 128, dtype=jnp.int32)]
        + [shape(row_spans[0][1] * batch + height, width)] * far_count,
        [table_slot, cover, ids, near_ids, *far_ids, tables],
        [SMEM] + [VMEM] * (owners + 2),
        scratch=[pltpu.SMEM((slots + 1,), jnp.int32)],
        mib=4,
        flops=1e9,
    )
    sends = call(
        tail_kernel,
        [shape(*array.shape) for array in sends],
        [shard, *sends],
        aliases={1 + i: i for i in range(far_count)},
        mib=1,
        flops=1e8,
    )
    far = [far_swap(sends)]
    again, *sends = call(
        functools.partial(far_kernel, row_spans[1], owners, pad),
        [shape(8, batch, dtype=jnp.int32)] + [shape(row_spans[1][1] * batch, width)] * far_count,
        [lines, tables],
        mib=4,
        flops=5e8,
    )
    far.append(far_swap(sends))
    features = (total + 1) * width
    (partner,) = call(
        functools.partial(partner_kernel, slots, pad),
        [shape(slots * batch + height, width)],
        [lines, again, tables, shard],
        mib=4,
        flops=5e8,
    )
    mine, down, up, cot, bias = call(
        functools.partial(near_kernel, owners, slots, pad),
        [
            shape(slots * batch, width),
            shape(features, rank),
            shape(rank, features),
            shape(batch, features),
            shape(-(-(total + 1) // 8) * 8, width, dtype=F32),
        ],
        [meta, lines, partner, tables]
        + [down_rank, up_rank, cotangent, cross_bias.reshape(-1, width)],
        [SMEM] + [VMEM] * 7,
        mib=6,
    )
    hot_rows = hot_ids.T
    near = [mine, swap(partner, 1)]

    (group,) = call(
        functools.partial(shards_kernel, owners),
        [shape(owners * height, width)],
        [shard, near[1], *far[0]],
        mib=1,
    )
    shards = [group]
    for mask in range(owners, blocks, owners):
        pairs = [(peer(b, mask, blocks), b) for b in range(blocks)]
        shards.append(lax.ppermute(group, "blk", pairs))

    counts, base = call(
        functools.partial(counts_kernel, owners, blocks),
        [
            shape(-(-blocks // owners) * owners * height, batch),
            shape(batch, width, dtype=F32),
        ],
        [group, hot_rows, dense],
        mib=2,
    )
    sums = [shape(batch, rank, dtype=F32)] * 2
    low, grad = call(
        functools.partial(sums_kernel, (0, slots), range(NEAR), slots),
        sums,
        [*near, down, up, cot],
        mib=6,
    )
    low, grad = call(
        functools.partial(sums_kernel, row_spans[0], range(NEAR, owners), slots),
        sums,
        [*far[0], down, up, cot, low, grad],
        mib=6,
    )
    front, low, grad, *sends = call(
        functools.partial(second_kernel, row_spans[1], grad_spans[0], owners, slots, blocks),
        [shape(batch, width), shape(batch, rank), shape(batch, rank)]
        + [shape(grad_spans[0][1] * batch, width)] * far_count,
        [*far[1], *shards, counts, base, low, grad, down, up, bias, cot],
        mib=6,
    )
    far_grads = [far_swap(sends)]
    sends = call(
        functools.partial(grads_kernel, grad_spans[1], range(NEAR, owners), slots),
        [shape(grad_spans[1][1] * batch, width)] * far_count,
        [low, grad, down, up, bias, cot, front],
        mib=6,
    )
    far_grads.append(far_swap(sends))
    near_grads = call(
        functools.partial(grads_kernel, (0, slots), range(NEAR), slots),
        [shape(slots * batch, width)] * NEAR,
        [low, grad, down, up, bias, cot, sends[0]],
        mib=6,
    )
    last_near = near_grads[0]
    near_grads = [near_grads[0], swap(near_grads[1], 1)]
    (crossed,) = call(
        functools.partial(crossed_kernel, row_spans, owners, slots),
        [shape(*cotangent.shape)],
        [meta, *near, *far[0], *far[1], front, low, up, bias, last_near],
        [SMEM] + [VMEM] * (NEAR + 2 * far_count + 5),
        scratch=[pltpu.VMEM((total, batch, width), BF16)],
        mib=6,
    )

    (first, count), later = grad_spans
    grads_shape = shape(1, slots, table_rows, width, dtype=F32)
    table_grad, rest = pl.pallas_call(
        functools.partial(scatter_kernel, grad_spans[0], later, owners, pad),
        out_shape=[grads_shape, shape(later[1], table_rows, width, dtype=F32)],
        in_specs=[VMEM] * (1 + owners),
        out_specs=[pl.BlockSpec(memory_space=pl.ANY), VMEM],
        scratch_shapes=[
            pltpu.VMEM((count, table_rows, width), F32),
            pltpu.SemaphoreType.DMA((count,)),
        ],
        compiler_params=pltpu.CompilerParams(vmem_limit_bytes=6 << 20),
        name="scatter",
    )(lines, *near_grads, *far_grads[0])
    table_grad = pl.pallas_call(
        functools.partial(last_kernel, later, owners, pad),
        out_shape=grads_shape,
        in_specs=[VMEM] * (2 + far_count) + [pl.BlockSpec(memory_space=pl.ANY)],
        out_specs=pl.BlockSpec(memory_space=pl.ANY),
        scratch_shapes=[
            pltpu.VMEM((later[1], table_rows, width), F32),
            pltpu.SemaphoreType.DMA((later[1],)),
        ],
        input_output_aliases={2 + far_count: 0},
        compiler_params=pltpu.CompilerParams(vmem_limit_bytes=6 << 20),
        name="last",
    )(lines, rest, *far_grads[1], table_grad)
    return crossed, table_grad


def solution(mesh):
    placed = (
        P("blk", None),
        P(("blk", "table"), None),
        P(("blk", "table"), None),
        P(("blk", "table"), None),
        P(),
        P("table", None, None),
        P(),
        P(),
        P(),
        P(("blk", "table"), None),
    )

    return jax.shard_map(
        on_device,
        mesh=mesh,
        in_specs=placed,
        out_specs=(P(("blk", "table"), None), P("blk", "table", None, None)),
        check_vma=False,
    )
```

```python
import functools

import jax
import jax.numpy as jnp
from jax import lax
from jax.experimental import pallas as pl
from jax.experimental.pallas import tpu as pltpu
from jax.sharding import PartitionSpec as P


BF16 = jnp.bfloat16
F32 = jnp.float32
ROW_PARTS = (3, 4)
GRAD_PARTS = (5, 2)
NEAR = 2
VMEM = pl.BlockSpec(memory_space=pltpu.VMEM)
SMEM = pl.BlockSpec(memory_space=pltpu.SMEM)
HBM = pl.BlockSpec(memory_space=pltpu.HBM)
OVER_LANES = (((1,), (1,)), ((), ()))


def peer(index, mask, count):
    return index ^ mask if count & (count - 1) == 0 else (index + mask) % count


def cut(slots, parts):
    whole = sum(parts)
    ends, total = [0], 0
    for part in parts:
        total += part
        ends.append(-(-slots * total // whole))
    return [(a, b - a) for a, b in zip(ends, ends[1:])]


def cover_kernel(out):
    out[...] = jnp.zeros_like(out)


def find(columns, tables, masks, span, pad, outs, batch):
    first, count = span
    rows = tables.shape[1]
    position = lax.broadcasted_iota(jnp.int32, (batch, rows), 1)
    for step in range(count):
        picks = [
            jnp.where(
                columns[:, k * pad + first + step : k * pad + first + step + 1] == position, 1.0, 0.0
            ).astype(BF16)
            for k in masks
        ]
        found = jnp.dot(
            jnp.concatenate(picks, axis=0), tables[first + step], preferred_element_type=F32
        ).astype(BF16)
        for i, out in enumerate(outs):
            out[step * batch : (step + 1) * batch, :] = found[i * batch : (i + 1) * batch]


def far_first_kernel(span, owners, slots, pad, *refs):
    slot_ref = refs[0]
    ids = refs[2 : 2 + owners]
    tables, lines, meta = refs[2 + owners : 5 + owners]
    outs, spots = refs[5 + owners : -1], refs[-1]
    batch = ids[0].shape[1]
    for slot in range(slots):
        spots[slot] = -1
    me = lax.axis_index("table")
    lane = lax.broadcasted_iota(jnp.int32, (1, meta.shape[1]), 1)
    table_at = jnp.full_like(lane, -1)
    place_of = jnp.zeros_like(lane)
    for table in range(slot_ref.shape[0]):
        slot = slot_ref[table]
        owner = slot // slots
        place = slot + ((owner ^ me) - owner) * slots
        spots[jnp.minimum(place, slots)] = table
        table_at = jnp.where(lane == place, table, table_at)
        place_of = jnp.where(lane == table, place, place_of)
    meta[0:1, :] = table_at
    meta[1:2, :] = place_of
    for slot in range(slots):
        table = spots[slot]
        for k in range(owners):
            line = ids[k][pl.ds(jnp.maximum(table, 0), 1), :]
            lines[k * pad + slot : k * pad + slot + 1, :] = jnp.where(table >= 0, line, -1)
    find(lines[...].T, tables, range(NEAR, owners), span, pad, outs, batch)


def tail_kernel(*refs):
    count = len(refs) // 2
    for out in refs[count + 1 :]:
        height = refs[0].shape[0]
        out[out.shape[0] - height :, :] = refs[0][...]


def far_kernel(span, owners, pad, lines, tables, again, *outs):
    again[...] = lines[0:8, :]
    find(lines[...].T, tables, range(NEAR, owners), span, pad, outs, lines.shape[1])


def partner_kernel(slots, pad, lines, _, tables, shard, out):
    batch = lines.shape[1]
    find(lines[...].T, tables, [1], (0, slots), pad, [out], batch)
    out[slots * batch : slots * batch + shard.shape[0], :] = shard[...]


def near_kernel(owners, slots, pad, *refs):
    meta, lines, _, tables, down_in, up_in, cot_in, bias_in = refs[:8]
    out, down, up, cot, bias = refs[8:]
    batch = lines.shape[1]
    width = bias.shape[1]
    for i in range(owners * slots + 1):
        spot = jnp.maximum(meta[0, i - 1], 0) + 1 if i else 0
        block = pl.ds(pl.multiple_of(spot * width, width), width) if i else slice(0, width)
        here = slice(i * width, (i + 1) * width)
        down[here, :] = down_in[block, :]
        up[:, here] = up_in[:, block]
        cot[:, here] = cot_in[:, block]
        bias[i : i + 1, :] = bias_in[pl.ds(spot, 1), :]
    find(lines[...].T, tables, [0], (0, slots), pad, [out], batch)


def shards_kernel(owners, *refs):
    shard, near = refs[:2]
    far, out = refs[2:owners], refs[owners]
    height, _ = shard.shape
    parts = [shard[...], near[near.shape[0] - height :, :]]
    parts += [ref[ref.shape[0] - height :, :] for ref in far]
    out[...] = jnp.concatenate(parts, axis=0)


def wide(ref, count, batch):
    return jnp.concatenate([ref[i * batch : (i + 1) * batch, :] for i in range(count)], axis=1)


def add_up(x, begin, down, up, cot, low, grad):
    span = slice(begin, begin + x.shape[1])
    mixed = (cot[:, span].astype(F32) * x.astype(F32)).astype(BF16)
    more = jnp.dot(x, down[span, :], preferred_element_type=F32)
    more_grad = lax.dot_general(mixed, up[:, span], OVER_LANES, preferred_element_type=F32)
    return (more, more_grad) if low is None else (low + more, grad + more_grad)


def grads_to(out, begin, count, low, grad, down, up, bias, cot):
    batch = cot.shape[0]
    width = bias.shape[1]
    span = slice(begin * width, (begin + count) * width)
    b = jnp.concatenate([bias[begin + i : begin + i + 1, :] for i in range(count)], axis=1)
    gate = jnp.dot(low, up[:, span], preferred_element_type=F32) + b
    back = lax.dot_general(grad, down[span, :], OVER_LANES, preferred_element_type=F32)
    result = (cot[:, span].astype(F32) * (gate + 1.0) + back).astype(BF16)
    for i in range(count):
        out[i * batch : (i + 1) * batch, :] = result[:, i * width : (i + 1) * width]


def sums_kernel(span, masks, slots, *refs):
    rows, refs = refs[: len(masks)], refs[len(masks) :]
    down, up, cot = refs[:3]
    low, grad = (ref[...] for ref in refs[3:5]) if len(refs) == 7 else (None, None)
    low_out, grad_out = refs[-2:]
    batch = cot.shape[0]
    width = rows[0].shape[1]
    for k, ref in zip(masks, rows):
        x = wide(ref, span[1], batch)
        low, grad = add_up(x, (1 + k * slots + span[0]) * width, down, up, cot, low, grad)
    low_out[...] = low
    grad_out[...] = grad


def counts_kernel(owners, blocks, group, hot_ids, dense, counts, base):
    batch = dense.shape[0]
    me = lax.axis_index("table")
    mine = lax.axis_index("blk")
    height = group.shape[0] // owners
    row = lax.broadcasted_iota(jnp.int32, (height, batch), 0)
    for part in range(-(-blocks // owners)):
        for k in range(owners):
            mask = part * owners + (me ^ k)
            first = jnp.where(mask < blocks, peer(mine, mask, blocks) * height, -height)
            total = jnp.zeros((height, batch), F32)
            for i in range(hot_ids.shape[0]):
                total += jnp.where(hot_ids[i : i + 1, :] - first == row, 1.0, 0.0)
            begin = (part * owners + k) * height
            counts[begin : begin + height, :] = total.astype(BF16)
    pooled = lax.dot_general(
        counts[: owners * height, :],
        group[...],
        (((0,), (0,)), ((), ())),
        preferred_element_type=F32,
    )
    base[...] = dense[...].astype(F32) + pooled


def second_kernel(span, grad_span, owners, slots, blocks, *refs):
    odds = range(NEAR + 1, owners, 2)
    far = refs[: len(odds)]
    refs = refs[len(odds) :]
    held = -(-blocks // owners)
    shards = refs[:held]
    counts, base, low_in, grad_in, down, up, bias, cot = refs[held : 8 + held]
    front_out, low_out, grad_out = refs[8 + held : 11 + held]
    outs = refs[11 + held :]
    batch, width = base.shape
    pooled = base[...]
    for part in range(1, held):
        rows = counts[part * shards[part].shape[0] : (part + 1) * shards[part].shape[0], :]
        pooled += lax.dot_general(
            rows, shards[part][...], (((0,), (0,)), ((), ())), preferred_element_type=F32
        )
    front = pooled.astype(BF16)
    front_out[...] = front
    low, grad = add_up(front, 0, down, up, cot, low_in[...], grad_in[...])
    for k, ref in zip(odds, far):
        x = wide(ref, span[1], batch)
        low, grad = add_up(x, (1 + k * slots + span[0]) * width, down, up, cot, low, grad)
    low = low.astype(BF16)
    grad = grad.astype(BF16)
    low_out[...] = low
    grad_out[...] = grad
    for k, out in zip(range(NEAR, owners, 2), outs):
        begin = 1 + k * slots + grad_span[0]
        grads_to(out, begin, grad_span[1], low, grad, down, up, bias, cot)


def grads_kernel(span, masks, slots, low, grad, down, up, bias, cot, _, *outs):
    for k, out in zip(masks, outs):
        begin = 1 + k * slots + span[0]
        grads_to(out, begin, span[1], low[...], grad[...], down, up, bias, cot)


def crossed_kernel(spans, owners, slots, *refs):
    meta = refs[0]
    chunks = len(spans)
    near = refs[1 : 1 + NEAR]
    count = owners - NEAR
    far = [refs[1 + NEAR + c * count : 1 + NEAR + (c + 1) * count] for c in range(chunks)]
    front, low, up, bias, _, out, held = refs[1 + NEAR + chunks * count :]
    batch, width = front.shape

    def gated(xs, begin):
        span = slice(begin * width, (begin + len(xs)) * width)
        gate = jnp.dot(low[...], up[:, span], preferred_element_type=F32)
        for i, x in enumerate(xs):
            part = gate[:, i * width : (i + 1) * width] + bias[begin + i : begin + i + 1, :]
            x = x.astype(F32)
            xs[i] = (x * part + x).astype(BF16)
        return xs

    out[:, :width] = gated([front[...]], 0)[0]
    runs = [(ref, k, 0, slots) for k, ref in enumerate(near)]
    runs += [(ref, k, *spans[c]) for c in range(chunks) for k, ref in enumerate(far[c], NEAR)]
    for ref, k, first, steps in runs:
        xs = [ref[i * batch : (i + 1) * batch, :] for i in range(steps)]
        for i, value in enumerate(gated(xs, 1 + k * slots + first)):
            held[k * slots + first + i] = value
    for table in range(out.shape[1] // width - 1):
        out[:, (table + 1) * width : (table + 2) * width] = held[meta[1, table]]


def summed(lines, masks, slot, grads, pad, rows):
    batch = lines.shape[1]
    position = lax.broadcasted_iota(jnp.int32, (rows, batch), 0)
    picks = [
        jnp.where(position == lines[k * pad + slot : k * pad + slot + 1, :], 1.0, 0.0).astype(BF16)
        for k in masks
    ]
    return jnp.dot(
        jnp.concatenate(picks, axis=1), jnp.concatenate(grads, axis=0), preferred_element_type=F32
    )


def scatter_kernel(span, later, owners, pad, *refs):
    lines = refs[0]
    near = refs[1 : 1 + NEAR]
    far = refs[1 + NEAR : 1 + owners]
    out, rest, held, sems = refs[1 + owners :]
    rows = out.shape[2]
    batch = lines.shape[1]
    first, count = span
    copies = []
    for step in range(count):
        slot = first + step
        grads = [ref[slot * batch : (slot + 1) * batch, :] for ref in near]
        grads += [ref[step * batch : (step + 1) * batch, :] for ref in far]
        held[step] = summed(lines, range(owners), slot, grads, pad, rows)
        copies.append(pltpu.make_async_copy(held.at[step], out.at[0, slot], sems.at[step]))
        copies[-1].start()
    for step in range(later[1]):
        slot = later[0] + step
        grads = [ref[slot * batch : (slot + 1) * batch, :] for ref in near]
        rest[step] = summed(lines, range(NEAR), slot, grads, pad, rows)
    for copy in copies:
        copy.wait()


def last_kernel(span, owners, pad, *refs):
    lines, rest = refs[:2]
    far = refs[2 : 2 + owners - NEAR]
    out, held, sems = refs[3 + owners - NEAR :]
    rows = out.shape[2]
    batch = lines.shape[1]
    copies = []
    for step in range(span[1]):
        slot = span[0] + step
        grads = [ref[step * batch : (step + 1) * batch, :] for ref in far]
        held[step] = rest[step] + summed(lines, range(NEAR, owners), slot, grads, pad, rows)
        copies.append(pltpu.make_async_copy(held.at[step], out.at[0, slot], sems.at[step]))
        copies[-1].start()
    for copy in copies:
        copy.wait()


def on_device(
    hot_slab,
    hot_ids,
    dense,
    cold_ids,
    table_slot,
    cold_tables,
    down_rank,
    up_rank,
    cross_bias,
    cotangent,
):
    batch, width = dense.shape
    owners = lax.axis_size("table")
    blocks = lax.axis_size("blk")
    slots, table_rows = cold_tables.shape[:2]
    rank = down_rank.shape[1]
    height = hot_slab.shape[0]
    total = owners * slots
    pad = -(-slots // 8) * 8
    row_spans, grad_spans = cut(slots, ROW_PARTS), cut(slots, GRAD_PARTS)
    assert owners & (owners - 1) == 0 and owners > NEAR
    far_count = owners - NEAR

    def call(kernel, shapes, operands, specs=None, *, mib, scratch=(), aliases=None, flops=4e9):
        return pl.pallas_call(
            kernel,
            out_shape=shapes,
            in_specs=[VMEM] * len(operands) if specs is None else specs,
            out_specs=[VMEM] * len(shapes),
            scratch_shapes=list(scratch),
            input_output_aliases=aliases or {},
            compiler_params=pltpu.CompilerParams(vmem_limit_bytes=mib << 20),
            cost_estimate=pl.CostEstimate(flops=int(flops), transcendentals=0, bytes_accessed=1 << 20),
        )(*operands)

    def swap(array, k):
        return lax.ppermute(array, "table", [(i, i ^ k) for i in range(owners)])

    def far_swap(arrays):
        return [swap(array, k) for k, array in enumerate(arrays, NEAR)]

    def shape(*dims, dtype=BF16):
        return jax.ShapeDtypeStruct(dims, dtype)

    ids = cold_ids.T
    far_ids = far_swap([ids] * far_count)
    near_ids = swap(ids, 1)
    shard = lax.ppermute(
        hot_slab,
        ("blk", "table"),
        [
            (peer(b, t, blocks) * owners + t, b * owners + t)
            for b in range(blocks)
            for t in range(owners)
        ],
    )
    (cover,) = call(cover_kernel, [shape(8, 128, dtype=jnp.int32)], [], mib=1)
    tables = cold_tables
    lines, meta, *sends = call(
        functools.partial(far_first_kernel, row_spans[0], owners, slots, pad),
        [shape(owners * pad, batch, dtype=jnp.int32), shape(8, 128, dtype=jnp.int32)]
        + [shape(row_spans[0][1] * batch + height, width)] * far_count,
        [table_slot, cover, ids, near_ids, *far_ids, tables],
        [SMEM] + [VMEM] * (owners + 2),
        scratch=[pltpu.SMEM((slots + 1,), jnp.int32)],
        mib=4,
        flops=1e9,
    )
    sends = call(
        tail_kernel,
        [shape(*array.shape) for array in sends],
        [shard, *sends],
        aliases={1 + i: i for i in range(far_count)},
        mib=1,
        flops=1e8,
    )
    far = [far_swap(sends)]
    again, *sends = call(
        functools.partial(far_kernel, row_spans[1], owners, pad),
        [shape(8, batch, dtype=jnp.int32)] + [shape(row_spans[1][1] * batch, width)] * far_count,
        [lines, tables],
        mib=4,
        flops=5e8,
    )
    far.append(far_swap(sends))
    features = (total + 1) * width
    (partner,) = call(
        functools.partial(partner_kernel, slots, pad),
        [shape(slots * batch + height, width)],
        [lines, again, tables, shard],
        mib=4,
        flops=5e8,
    )
    mine, down, up, cot, bias = call(
        functools.partial(near_kernel, owners, slots, pad),
        [
            shape(slots * batch, width),
            shape(features, rank),
            shape(rank, features),
            shape(batch, features),
            shape(-(-(total + 1) // 8) * 8, width, dtype=F32),
        ],
        [meta, lines, partner, tables]
        + [down_rank, up_rank, cotangent, cross_bias.reshape(-1, width)],
        [SMEM] + [VMEM] * 7,
        mib=6,
    )
    hot_rows = hot_ids.T
    near = [mine, swap(partner, 1)]

    (group,) = call(
        functools.partial(shards_kernel, owners),
        [shape(owners * height, width)],
        [shard, near[1], *far[0]],
        mib=1,
    )
    shards = [group]
    for mask in range(owners, blocks, owners):
        pairs = [(peer(b, mask, blocks), b) for b in range(blocks)]
        shards.append(lax.ppermute(group, "blk", pairs))

    counts, base = call(
        functools.partial(counts_kernel, owners, blocks),
        [
            shape(-(-blocks // owners) * owners * height, batch),
            shape(batch, width, dtype=F32),
        ],
        [group, hot_rows, dense],
        mib=2,
    )
    sums = [shape(batch, rank, dtype=F32)] * 2
    low, grad = call(
        functools.partial(sums_kernel, (0, slots), range(NEAR), slots),
        sums,
        [*near, down, up, cot],
        mib=6,
    )
    low, grad = call(
        functools.partial(sums_kernel, row_spans[0], range(NEAR, owners), slots),
        sums,
        [*far[0], down, up, cot, low, grad],
        mib=6,
    )
    low, grad = call(
        functools.partial(sums_kernel, row_spans[1], range(NEAR, owners, 2), slots),
        sums,
        [*far[1][::2], down, up, cot, low, grad],
        mib=6,
    )
    front, low, grad, *sends = call(
        functools.partial(second_kernel, row_spans[1], grad_spans[0], owners, slots, blocks),
        [shape(batch, width), shape(batch, rank), shape(batch, rank)]
        + [shape(grad_spans[0][1] * batch, width)] * (far_count // 2),
        [*far[1][1::2], *shards, counts, base, low, grad, down, up, bias, cot],
        mib=6,
    )
    odds = call(
        functools.partial(grads_kernel, grad_spans[0], range(NEAR + 1, owners, 2), slots),
        [shape(grad_spans[0][1] * batch, width)] * (far_count // 2),
        [low, grad, down, up, bias, cot, front],
        mib=6,
    )
    sends = [array for pair in zip(sends, odds) for array in pair]
    far_grads = [far_swap(sends)]
    sends = call(
        functools.partial(grads_kernel, grad_spans[1], range(NEAR, owners), slots),
        [shape(grad_spans[1][1] * batch, width)] * far_count,
        [low, grad, down, up, bias, cot, front],
        mib=6,
    )
    far_grads.append(far_swap(sends))
    near_grads = call(
        functools.partial(grads_kernel, (0, slots), range(NEAR), slots),
        [shape(slots * batch, width)] * NEAR,
        [low, grad, down, up, bias, cot, sends[0]],
        mib=6,
    )
    last_near = near_grads[0]
    near_grads = [near_grads[0], swap(near_grads[1], 1)]
    (crossed,) = call(
        functools.partial(crossed_kernel, row_spans, owners, slots),
        [shape(*cotangent.shape)],
        [meta, *near, *far[0], *far[1], front, low, up, bias, last_near],
        [SMEM] + [VMEM] * (NEAR + 2 * far_count + 5),
        scratch=[pltpu.VMEM((total, batch, width), BF16)],
        mib=6,
    )

    (first, count), later = grad_spans
    grads_shape = shape(1, slots, table_rows, width, dtype=F32)
    table_grad, rest = pl.pallas_call(
        functools.partial(scatter_kernel, grad_spans[0], later, owners, pad),
        out_shape=[grads_shape, shape(later[1], table_rows, width, dtype=F32)],
        in_specs=[VMEM] * (1 + owners),
        out_specs=[pl.BlockSpec(memory_space=pl.ANY), VMEM],
        scratch_shapes=[
            pltpu.VMEM((count, table_rows, width), F32),
            pltpu.SemaphoreType.DMA((count,)),
        ],
        compiler_params=pltpu.CompilerParams(vmem_limit_bytes=6 << 20),
        name="scatter",
    )(lines, *near_grads, *far_grads[0])
    table_grad = pl.pallas_call(
        functools.partial(last_kernel, later, owners, pad),
        out_shape=grads_shape,
        in_specs=[VMEM] * (2 + far_count) + [pl.BlockSpec(memory_space=pl.ANY)],
        out_specs=pl.BlockSpec(memory_space=pl.ANY),
        scratch_shapes=[
            pltpu.VMEM((later[1], table_rows, width), F32),
            pltpu.SemaphoreType.DMA((later[1],)),
        ],
        input_output_aliases={2 + far_count: 0},
        compiler_params=pltpu.CompilerParams(vmem_limit_bytes=6 << 20),
        name="last",
    )(lines, rest, *far_grads[1], table_grad)
    return crossed, table_grad


def solution(mesh):
    placed = (
        P("blk", None),
        P(("blk", "table"), None),
        P(("blk", "table"), None),
        P(("blk", "table"), None),
        P(),
        P("table", None, None),
        P(),
        P(),
        P(),
        P(("blk", "table"), None),
    )

    return jax.shard_map(
        on_device,
        mesh=mesh,
        in_specs=placed,
        out_specs=(P(("blk", "table"), None), P("blk", "table", None, None)),
        check_vma=False,
    )
```

```python
import functools

import jax
import jax.numpy as jnp
from jax import lax
from jax.experimental import pallas as pl
from jax.experimental.pallas import tpu as pltpu
from jax.sharding import PartitionSpec as P


BF16 = jnp.bfloat16
F32 = jnp.float32
ROW_PARTS = (3, 4)
GRAD_PARTS = (5, 2)
NEAR = 2
VMEM = pl.BlockSpec(memory_space=pltpu.VMEM)
SMEM = pl.BlockSpec(memory_space=pltpu.SMEM)
HBM = pl.BlockSpec(memory_space=pltpu.HBM)
OVER_LANES = (((1,), (1,)), ((), ()))


def peer(index, mask, count):
    return index ^ mask if count & (count - 1) == 0 else (index + mask) % count


def cut(slots, parts):
    whole = sum(parts)
    ends, total = [0], 0
    for part in parts:
        total += part
        ends.append(-(-slots * total // whole))
    return [(a, b - a) for a, b in zip(ends, ends[1:])]


def cover_kernel(out):
    out[...] = jnp.zeros_like(out)


def find(columns, tables, masks, span, pad, outs, batch):
    first, count = span
    rows = tables.shape[1]
    position = lax.broadcasted_iota(jnp.int32, (batch, rows), 1)
    for step in range(count):
        picks = [
            jnp.where(
                columns[:, k * pad + first + step : k * pad + first + step + 1] == position, 1.0, 0.0
            ).astype(BF16)
            for k in masks
        ]
        found = jnp.dot(
            jnp.concatenate(picks, axis=0), tables[first + step], preferred_element_type=F32
        ).astype(BF16)
        for i, out in enumerate(outs):
            out[step * batch : (step + 1) * batch, :] = found[i * batch : (i + 1) * batch]


def far_first_kernel(span, owners, slots, pad, *refs):
    slot_ref = refs[0]
    ids = refs[2 : 2 + owners]
    tables, lines, meta = refs[2 + owners : 5 + owners]
    outs, spots = refs[5 + owners : -1], refs[-1]
    batch = ids[0].shape[1]
    for slot in range(slots):
        spots[slot] = -1
    me = lax.axis_index("table")
    lane = lax.broadcasted_iota(jnp.int32, (1, meta.shape[1]), 1)
    table_at = jnp.full_like(lane, -1)
    place_of = jnp.zeros_like(lane)
    for table in range(slot_ref.shape[0]):
        slot = slot_ref[table]
        owner = slot // slots
        place = slot + ((owner ^ me) - owner) * slots
        spots[jnp.minimum(place, slots)] = table
        table_at = jnp.where(lane == place, table, table_at)
        place_of = jnp.where(lane == table, place, place_of)
    meta[0:1, :] = table_at
    meta[1:2, :] = place_of
    for slot in range(slots):
        table = spots[slot]
        for k in range(owners):
            line = ids[k][pl.ds(jnp.maximum(table, 0), 1), :]
            lines[k * pad + slot : k * pad + slot + 1, :] = jnp.where(table >= 0, line, -1)
    find(lines[...].T, tables, range(NEAR, owners), span, pad, outs, batch)


def tail_kernel(*refs):
    count = len(refs) // 2
    for out in refs[count + 1 :]:
        height = refs[0].shape[0]
        out[out.shape[0] - height :, :] = refs[0][...]


def far_kernel(span, owners, pad, lines, tables, again, *outs):
    again[...] = lines[0:8, :]
    find(lines[...].T, tables, range(NEAR, owners), span, pad, outs, lines.shape[1])


def partner_kernel(slots, pad, lines, _, tables, shard, out):
    batch = lines.shape[1]
    find(lines[...].T, tables, [1], (0, slots), pad, [out], batch)
    out[slots * batch : slots * batch + shard.shape[0], :] = shard[...]


def near_kernel(owners, slots, pad, *refs):
    meta, lines, _, tables, down_in, up_in, cot_in, bias_in = refs[:8]
    out, down, up, cot, bias = refs[8:]
    batch = lines.shape[1]
    width = bias.shape[1]
    for i in range(owners * slots + 1):
        spot = jnp.maximum(meta[0, i - 1], 0) + 1 if i else 0
        block = pl.ds(pl.multiple_of(spot * width, width), width) if i else slice(0, width)
        here = slice(i * width, (i + 1) * width)
        down[here, :] = down_in[block, :]
        up[:, here] = up_in[:, block]
        cot[:, here] = cot_in[:, block]
        bias[i : i + 1, :] = bias_in[pl.ds(spot, 1), :]
    find(lines[...].T, tables, [0], (0, slots), pad, [out], batch)


def shards_kernel(owners, *refs):
    shard, near = refs[:2]
    far, out = refs[2:owners], refs[owners]
    height, _ = shard.shape
    parts = [shard[...], near[near.shape[0] - height :, :]]
    parts += [ref[ref.shape[0] - height :, :] for ref in far]
    out[...] = jnp.concatenate(parts, axis=0)


def wide(ref, count, batch):
    return jnp.concatenate([ref[i * batch : (i + 1) * batch, :] for i in range(count)], axis=1)


def add_up(x, begin, down, up, cot, low, grad):
    span = slice(begin, begin + x.shape[1])
    mixed = (cot[:, span].astype(F32) * x.astype(F32)).astype(BF16)
    more = jnp.dot(x, down[span, :], preferred_element_type=F32)
    more_grad = lax.dot_general(mixed, up[:, span], OVER_LANES, preferred_element_type=F32)
    return (more, more_grad) if low is None else (low + more, grad + more_grad)


def grads_to(out, begin, count, low, grad, down, up, bias, cot):
    batch = cot.shape[0]
    width = bias.shape[1]
    span = slice(begin * width, (begin + count) * width)
    b = jnp.concatenate([bias[begin + i : begin + i + 1, :] for i in range(count)], axis=1)
    gate = jnp.dot(low, up[:, span], preferred_element_type=F32) + b
    back = lax.dot_general(grad, down[span, :], OVER_LANES, preferred_element_type=F32)
    result = (cot[:, span].astype(F32) * (gate + 1.0) + back).astype(BF16)
    for i in range(count):
        out[i * batch : (i + 1) * batch, :] = result[:, i * width : (i + 1) * width]


def sums_kernel(span, masks, slots, *refs):
    rows, refs = refs[: len(masks)], refs[len(masks) :]
    down, up, cot = refs[:3]
    low, grad = (ref[...] for ref in refs[3:5]) if len(refs) == 7 else (None, None)
    low_out, grad_out = refs[-2:]
    batch = cot.shape[0]
    width = rows[0].shape[1]
    for k, ref in zip(masks, rows):
        x = wide(ref, span[1], batch)
        low, grad = add_up(x, (1 + k * slots + span[0]) * width, down, up, cot, low, grad)
    low_out[...] = low
    grad_out[...] = grad


def counts_kernel(owners, blocks, group, hot_ids, dense, counts, base):
    batch = dense.shape[0]
    me = lax.axis_index("table")
    mine = lax.axis_index("blk")
    height = group.shape[0] // owners
    row = lax.broadcasted_iota(jnp.int32, (height, batch), 0)
    for part in range(-(-blocks // owners)):
        for k in range(owners):
            mask = part * owners + (me ^ k)
            first = jnp.where(mask < blocks, peer(mine, mask, blocks) * height, -height)
            total = jnp.zeros((height, batch), F32)
            for i in range(hot_ids.shape[0]):
                total += jnp.where(hot_ids[i : i + 1, :] - first == row, 1.0, 0.0)
            begin = (part * owners + k) * height
            counts[begin : begin + height, :] = total.astype(BF16)
    pooled = lax.dot_general(
        counts[: owners * height, :],
        group[...],
        (((0,), (0,)), ((), ())),
        preferred_element_type=F32,
    )
    base[...] = dense[...].astype(F32) + pooled


def second_kernel(span, grad_span, owners, slots, blocks, *refs):
    odds = range(NEAR + 1, owners, 2)
    far = refs[: len(odds)]
    refs = refs[len(odds) :]
    held = -(-blocks // owners)
    shards = refs[:held]
    counts, base, low_in, grad_in, down, up, bias, cot = refs[held : 8 + held]
    front_out, low_out, grad_out = refs[8 + held : 11 + held]
    outs = refs[11 + held :]
    batch, width = base.shape
    pooled = base[...]
    for part in range(1, held):
        rows = counts[part * shards[part].shape[0] : (part + 1) * shards[part].shape[0], :]
        pooled += lax.dot_general(
            rows, shards[part][...], (((0,), (0,)), ((), ())), preferred_element_type=F32
        )
    front = pooled.astype(BF16)
    front_out[...] = front
    low, grad = add_up(front, 0, down, up, cot, low_in[...], grad_in[...])
    for k, ref in zip(odds, far):
        x = wide(ref, span[1], batch)
        low, grad = add_up(x, (1 + k * slots + span[0]) * width, down, up, cot, low, grad)
    low = low.astype(BF16)
    grad = grad.astype(BF16)
    low_out[...] = low
    grad_out[...] = grad
    for k, out in zip(range(NEAR, owners, 2), outs):
        begin = 1 + k * slots + grad_span[0]
        grads_to(out, begin, grad_span[1], low, grad, down, up, bias, cot)


def grads_kernel(span, masks, slots, low, grad, down, up, bias, cot, _, *outs):
    for k, out in zip(masks, outs):
        begin = 1 + k * slots + span[0]
        grads_to(out, begin, span[1], low[...], grad[...], down, up, bias, cot)


def crossed_kernel(spans, owners, slots, *refs):
    meta = refs[0]
    chunks = len(spans)
    near = refs[1 : 1 + NEAR]
    count = owners - NEAR
    far = [refs[1 + NEAR + c * count : 1 + NEAR + (c + 1) * count] for c in range(chunks)]
    front, low, up, bias, _, out, held = refs[1 + NEAR + chunks * count :]
    batch, width = front.shape

    def gated(xs, begin):
        span = slice(begin * width, (begin + len(xs)) * width)
        gate = jnp.dot(low[...], up[:, span], preferred_element_type=F32)
        for i, x in enumerate(xs):
            part = gate[:, i * width : (i + 1) * width] + bias[begin + i : begin + i + 1, :]
            x = x.astype(F32)
            xs[i] = (x * part + x).astype(BF16)
        return xs

    out[:, :width] = gated([front[...]], 0)[0]
    runs = [(ref, k, 0, slots) for k, ref in enumerate(near)]
    runs += [(ref, k, *spans[c]) for c in range(chunks) for k, ref in enumerate(far[c], NEAR)]
    for ref, k, first, steps in runs:
        xs = [ref[i * batch : (i + 1) * batch, :] for i in range(steps)]
        for i, value in enumerate(gated(xs, 1 + k * slots + first)):
            held[k * slots + first + i] = value
    for table in range(out.shape[1] // width - 1):
        out[:, (table + 1) * width : (table + 2) * width] = held[meta[1, table]]


def summed(lines, masks, slot, grads, pad, rows):
    batch = lines.shape[1]
    position = lax.broadcasted_iota(jnp.int32, (rows, batch), 0)
    picks = [
        jnp.where(position == lines[k * pad + slot : k * pad + slot + 1, :], 1.0, 0.0).astype(BF16)
        for k in masks
    ]
    return jnp.dot(
        jnp.concatenate(picks, axis=1), jnp.concatenate(grads, axis=0), preferred_element_type=F32
    )


def near_scatter_kernel(slots, pad, *refs):
    lines = refs[0]
    near, out = refs[1:-1], refs[-1]
    batch = lines.shape[1]
    for slot in range(slots):
        grads = [ref[slot * batch : (slot + 1) * batch, :] for ref in near]
        out[slot] = summed(lines, range(NEAR), slot, grads, pad, out.shape[1])


def far_scatter_kernel(span, owners, pad, *refs):
    lines, near = refs[:2]
    far = refs[2 : 2 + owners - NEAR]
    out, held, sems = refs[-3:]
    rows = out.shape[2]
    batch = lines.shape[1]
    copies = []
    for step in range(span[1]):
        slot = span[0] + step
        grads = [ref[step * batch : (step + 1) * batch, :] for ref in far]
        held[step] = near[slot] + summed(lines, range(NEAR, owners), slot, grads, pad, rows)
        copies.append(pltpu.make_async_copy(held.at[step], out.at[0, slot], sems.at[step]))
        copies[-1].start()
    for copy in copies:
        copy.wait()


def on_device(
    hot_slab,
    hot_ids,
    dense,
    cold_ids,
    table_slot,
    cold_tables,
    down_rank,
    up_rank,
    cross_bias,
    cotangent,
):
    batch, width = dense.shape
    owners = lax.axis_size("table")
    blocks = lax.axis_size("blk")
    slots, table_rows = cold_tables.shape[:2]
    rank = down_rank.shape[1]
    height = hot_slab.shape[0]
    total = owners * slots
    pad = -(-slots // 8) * 8
    row_spans, grad_spans = cut(slots, ROW_PARTS), cut(slots, GRAD_PARTS)
    assert owners & (owners - 1) == 0 and owners > NEAR
    far_count = owners - NEAR

    def call(kernel, shapes, operands, specs=None, *, mib, scratch=(), aliases=None, flops=4e9):
        return pl.pallas_call(
            kernel,
            out_shape=shapes,
            in_specs=[VMEM] * len(operands) if specs is None else specs,
            out_specs=[VMEM] * len(shapes),
            scratch_shapes=list(scratch),
            input_output_aliases=aliases or {},
            compiler_params=pltpu.CompilerParams(vmem_limit_bytes=mib << 20),
            cost_estimate=pl.CostEstimate(flops=int(flops), transcendentals=0, bytes_accessed=1 << 20),
        )(*operands)

    def swap(array, k):
        return lax.ppermute(array, "table", [(i, i ^ k) for i in range(owners)])

    def far_swap(arrays):
        return [swap(array, k) for k, array in enumerate(arrays, NEAR)]

    def shape(*dims, dtype=BF16):
        return jax.ShapeDtypeStruct(dims, dtype)

    ids = cold_ids.T
    far_ids = far_swap([ids] * far_count)
    near_ids = swap(ids, 1)
    shard = lax.ppermute(
        hot_slab,
        ("blk", "table"),
        [
            (peer(b, t, blocks) * owners + t, b * owners + t)
            for b in range(blocks)
            for t in range(owners)
        ],
    )
    (cover,) = call(cover_kernel, [shape(8, 128, dtype=jnp.int32)], [], mib=1)
    tables = cold_tables
    lines, meta, *sends = call(
        functools.partial(far_first_kernel, row_spans[0], owners, slots, pad),
        [shape(owners * pad, batch, dtype=jnp.int32), shape(8, 128, dtype=jnp.int32)]
        + [shape(row_spans[0][1] * batch + height, width)] * far_count,
        [table_slot, cover, ids, near_ids, *far_ids, tables],
        [SMEM] + [VMEM] * (owners + 2),
        scratch=[pltpu.SMEM((slots + 1,), jnp.int32)],
        mib=4,
        flops=1e9,
    )
    sends = call(
        tail_kernel,
        [shape(*array.shape) for array in sends],
        [shard, *sends],
        aliases={1 + i: i for i in range(far_count)},
        mib=1,
        flops=1e8,
    )
    far = [far_swap(sends)]
    again, *sends = call(
        functools.partial(far_kernel, row_spans[1], owners, pad),
        [shape(8, batch, dtype=jnp.int32)] + [shape(row_spans[1][1] * batch, width)] * far_count,
        [lines, tables],
        mib=4,
        flops=5e8,
    )
    far.append(far_swap(sends))
    features = (total + 1) * width
    (partner,) = call(
        functools.partial(partner_kernel, slots, pad),
        [shape(slots * batch + height, width)],
        [lines, again, tables, shard],
        mib=4,
        flops=5e8,
    )
    mine, down, up, cot, bias = call(
        functools.partial(near_kernel, owners, slots, pad),
        [
            shape(slots * batch, width),
            shape(features, rank),
            shape(rank, features),
            shape(batch, features),
            shape(-(-(total + 1) // 8) * 8, width, dtype=F32),
        ],
        [meta, lines, partner, tables]
        + [down_rank, up_rank, cotangent, cross_bias.reshape(-1, width)],
        [SMEM] + [VMEM] * 7,
        mib=6,
    )
    hot_rows = hot_ids.T
    near = [mine, swap(partner, 1)]

    (group,) = call(
        functools.partial(shards_kernel, owners),
        [shape(owners * height, width)],
        [shard, near[1], *far[0]],
        mib=1,
    )
    shards = [group]
    for mask in range(owners, blocks, owners):
        pairs = [(peer(b, mask, blocks), b) for b in range(blocks)]
        shards.append(lax.ppermute(group, "blk", pairs))

    counts, base = call(
        functools.partial(counts_kernel, owners, blocks),
        [
            shape(-(-blocks // owners) * owners * height, batch),
            shape(batch, width, dtype=F32),
        ],
        [group, hot_rows, dense],
        mib=2,
    )
    sums = [shape(batch, rank, dtype=F32)] * 2
    low, grad = call(
        functools.partial(sums_kernel, (0, slots), range(NEAR), slots),
        sums,
        [*near, down, up, cot],
        mib=6,
    )
    low, grad = call(
        functools.partial(sums_kernel, row_spans[0], range(NEAR, owners), slots),
        sums,
        [*far[0], down, up, cot, low, grad],
        mib=6,
    )
    low, grad = call(
        functools.partial(sums_kernel, row_spans[1], range(NEAR, owners, 2), slots),
        sums,
        [*far[1][::2], down, up, cot, low, grad],
        mib=6,
    )
    front, low, grad, *sends = call(
        functools.partial(second_kernel, row_spans[1], grad_spans[0], owners, slots, blocks),
        [shape(batch, width), shape(batch, rank), shape(batch, rank)]
        + [shape(grad_spans[0][1] * batch, width)] * (far_count // 2),
        [*far[1][1::2], *shards, counts, base, low, grad, down, up, bias, cot],
        mib=6,
    )
    odds = call(
        functools.partial(grads_kernel, grad_spans[0], range(NEAR + 1, owners, 2), slots),
        [shape(grad_spans[0][1] * batch, width)] * (far_count // 2),
        [low, grad, down, up, bias, cot, front],
        mib=6,
    )
    sends = [array for pair in zip(sends, odds) for array in pair]
    far_grads = [far_swap(sends)]
    sends = call(
        functools.partial(grads_kernel, grad_spans[1], range(NEAR, owners), slots),
        [shape(grad_spans[1][1] * batch, width)] * far_count,
        [low, grad, down, up, bias, cot, front],
        mib=6,
    )
    far_grads.append(far_swap(sends))
    near_grads = call(
        functools.partial(grads_kernel, (0, slots), range(NEAR), slots),
        [shape(slots * batch, width)] * NEAR,
        [low, grad, down, up, bias, cot, sends[0]],
        mib=6,
    )
    last_near = near_grads[0]
    near_grads = [near_grads[0], swap(near_grads[1], 1)]
    (crossed,) = call(
        functools.partial(crossed_kernel, row_spans, owners, slots),
        [shape(*cotangent.shape)],
        [meta, *near, *far[0], *far[1], front, low, up, bias, last_near],
        [SMEM] + [VMEM] * (NEAR + 2 * far_count + 5),
        scratch=[pltpu.VMEM((total, batch, width), BF16)],
        mib=6,
    )

    (near_sums,) = call(
        functools.partial(near_scatter_kernel, slots, pad),
        [shape(slots, table_rows, width, dtype=F32)],
        [lines, *near_grads],
        mib=6,
    )
    table_grad = []
    for chunk, (first, count) in enumerate(grad_spans):
        table_grad = [
            pl.pallas_call(
                functools.partial(far_scatter_kernel, (first, count), owners, pad),
                out_shape=shape(1, slots, table_rows, width, dtype=F32),
                in_specs=[VMEM] * (2 + far_count)
                + [pl.BlockSpec(memory_space=pl.ANY)] * len(table_grad),
                out_specs=pl.BlockSpec(memory_space=pl.ANY),
                scratch_shapes=[
                    pltpu.VMEM((count, table_rows, width), F32),
                    pltpu.SemaphoreType.DMA((count,)),
                ],
                input_output_aliases={2 + far_count: 0} if table_grad else {},
                compiler_params=pltpu.CompilerParams(vmem_limit_bytes=6 << 20),
            )(lines, near_sums, *far_grads[chunk], *table_grad)
        ]
    (table_grad,) = table_grad
    return crossed, table_grad


def solution(mesh):
    placed = (
        P("blk", None),
        P(("blk", "table"), None),
        P(("blk", "table"), None),
        P(("blk", "table"), None),
        P(),
        P("table", None, None),
        P(),
        P(),
        P(),
        P(("blk", "table"), None),
    )

    return jax.shard_map(
        on_device,
        mesh=mesh,
        in_specs=placed,
        out_specs=(P(("blk", "table"), None), P("blk", "table", None, None)),
        check_vma=False,
    )
```

```python
import functools

import jax
import jax.numpy as jnp
from jax import lax
from jax.experimental import pallas as pl
from jax.experimental.pallas import tpu as pltpu
from jax.sharding import PartitionSpec as P


BF16 = jnp.bfloat16
F32 = jnp.float32
ROW_PARTS = (3, 4)
GRAD_PARTS = (5, 2)
NEAR = 2
VMEM = pl.BlockSpec(memory_space=pltpu.VMEM)
SMEM = pl.BlockSpec(memory_space=pltpu.SMEM)
HBM = pl.BlockSpec(memory_space=pltpu.HBM)
OVER_LANES = (((1,), (1,)), ((), ()))


def peer(index, mask, count):
    return index ^ mask if count & (count - 1) == 0 else (index + mask) % count


def cut(slots, parts):
    whole = sum(parts)
    ends, total = [0], 0
    for part in parts:
        total += part
        ends.append(-(-slots * total // whole))
    return [(a, b - a) for a, b in zip(ends, ends[1:])]


def cover_kernel(out):
    out[...] = jnp.zeros_like(out)


def find(columns, tables, masks, span, pad, outs, batch):
    first, count = span
    rows = tables.shape[1]
    position = lax.broadcasted_iota(jnp.int32, (batch, rows), 1)
    for step in range(count):
        picks = [
            jnp.where(
                columns[:, k * pad + first + step : k * pad + first + step + 1] == position, 1.0, 0.0
            ).astype(BF16)
            for k in masks
        ]
        found = jnp.dot(
            jnp.concatenate(picks, axis=0), tables[first + step], preferred_element_type=F32
        ).astype(BF16)
        for i, out in enumerate(outs):
            out[step * batch : (step + 1) * batch, :] = found[i * batch : (i + 1) * batch]


def far_first_kernel(span, owners, slots, pad, *refs):
    slot_ref = refs[0]
    ids = refs[2 : 2 + owners]
    tables, lines, meta = refs[2 + owners : 5 + owners]
    outs, spots = refs[5 + owners : -1], refs[-1]
    batch = ids[0].shape[1]
    for slot in range(slots):
        spots[slot] = -1
    me = lax.axis_index("table")
    lane = lax.broadcasted_iota(jnp.int32, (1, meta.shape[1]), 1)
    table_at = jnp.full_like(lane, -1)
    place_of = jnp.zeros_like(lane)
    for table in range(slot_ref.shape[0]):
        slot = slot_ref[table]
        owner = slot // slots
        place = slot + ((owner ^ me) - owner) * slots
        spots[jnp.minimum(place, slots)] = table
        table_at = jnp.where(lane == place, table, table_at)
        place_of = jnp.where(lane == table, place, place_of)
    meta[0:1, :] = table_at
    meta[1:2, :] = place_of
    for slot in range(slots):
        table = spots[slot]
        for k in range(owners):
            line = ids[k][pl.ds(jnp.maximum(table, 0), 1), :]
            lines[k * pad + slot : k * pad + slot + 1, :] = jnp.where(table >= 0, line, -1)
    find(lines[...].T, tables, range(NEAR, owners), span, pad, outs, batch)


def tail_kernel(*refs):
    count = len(refs) // 2
    for out in refs[count + 1 :]:
        height = refs[0].shape[0]
        out[out.shape[0] - height :, :] = refs[0][...]


def far_kernel(span, owners, pad, lines, tables, again, *outs):
    again[...] = lines[0:8, :]
    find(lines[...].T, tables, range(NEAR, owners), span, pad, outs, lines.shape[1])


def partner_kernel(slots, pad, lines, _, tables, shard, out):
    batch = lines.shape[1]
    find(lines[...].T, tables, [1], (0, slots), pad, [out], batch)
    out[slots * batch : slots * batch + shard.shape[0], :] = shard[...]


def near_kernel(owners, slots, pad, *refs):
    meta, lines, _, tables, down_in, up_in, cot_in, bias_in = refs[:8]
    out, down, up, cot, bias = refs[8:]
    batch = lines.shape[1]
    width = bias.shape[1]
    for i in range(owners * slots + 1):
        spot = jnp.maximum(meta[0, i - 1], 0) + 1 if i else 0
        block = pl.ds(pl.multiple_of(spot * width, width), width) if i else slice(0, width)
        here = slice(i * width, (i + 1) * width)
        down[here, :] = down_in[block, :]
        up[:, here] = up_in[:, block]
        cot[:, here] = cot_in[:, block]
        bias[i : i + 1, :] = bias_in[pl.ds(spot, 1), :]
    find(lines[...].T, tables, [0], (0, slots), pad, [out], batch)


def shards_kernel(owners, *refs):
    shard, near = refs[:2]
    far, out = refs[2:owners], refs[owners]
    height, _ = shard.shape
    parts = [shard[...], near[near.shape[0] - height :, :]]
    parts += [ref[ref.shape[0] - height :, :] for ref in far]
    out[...] = jnp.concatenate(parts, axis=0)


def wide(ref, count, batch):
    return jnp.concatenate([ref[i * batch : (i + 1) * batch, :] for i in range(count)], axis=1)


def add_up(x, begin, down, up, cot, low, grad):
    span = slice(begin, begin + x.shape[1])
    mixed = (cot[:, span].astype(F32) * x.astype(F32)).astype(BF16)
    more = jnp.dot(x, down[span, :], preferred_element_type=F32)
    more_grad = lax.dot_general(mixed, up[:, span], OVER_LANES, preferred_element_type=F32)
    return (more, more_grad) if low is None else (low + more, grad + more_grad)


def grads_to(out, begin, count, low, grad, down, up, bias, cot):
    batch = cot.shape[0]
    width = bias.shape[1]
    span = slice(begin * width, (begin + count) * width)
    b = jnp.concatenate([bias[begin + i : begin + i + 1, :] for i in range(count)], axis=1)
    gate = jnp.dot(low, up[:, span], preferred_element_type=F32) + b
    back = lax.dot_general(grad, down[span, :], OVER_LANES, preferred_element_type=F32)
    result = (cot[:, span].astype(F32) * (gate + 1.0) + back).astype(BF16)
    for i in range(count):
        out[i * batch : (i + 1) * batch, :] = result[:, i * width : (i + 1) * width]


def sums_kernel(span, masks, slots, *refs):
    rows, refs = refs[: len(masks)], refs[len(masks) :]
    down, up, cot = refs[:3]
    low, grad = (ref[...] for ref in refs[3:5]) if len(refs) == 7 else (None, None)
    low_out, grad_out = refs[-2:]
    batch = cot.shape[0]
    width = rows[0].shape[1]
    for k, ref in zip(masks, rows):
        x = wide(ref, span[1], batch)
        low, grad = add_up(x, (1 + k * slots + span[0]) * width, down, up, cot, low, grad)
    low_out[...] = low
    grad_out[...] = grad


def counts_kernel(owners, blocks, group, hot_ids, dense, counts, base):
    batch = dense.shape[0]
    me = lax.axis_index("table")
    mine = lax.axis_index("blk")
    height = group.shape[0] // owners
    row = lax.broadcasted_iota(jnp.int32, (height, batch), 0)
    for part in range(-(-blocks // owners)):
        for k in range(owners):
            mask = part * owners + (me ^ k)
            first = jnp.where(mask < blocks, peer(mine, mask, blocks) * height, -height)
            total = jnp.zeros((height, batch), F32)
            for i in range(hot_ids.shape[0]):
                total += jnp.where(hot_ids[i : i + 1, :] - first == row, 1.0, 0.0)
            begin = (part * owners + k) * height
            counts[begin : begin + height, :] = total.astype(BF16)
    pooled = lax.dot_general(
        counts[: owners * height, :],
        group[...],
        (((0,), (0,)), ((), ())),
        preferred_element_type=F32,
    )
    base[...] = dense[...].astype(F32) + pooled


def second_kernel(span, grad_span, owners, slots, blocks, *refs):
    odds = range(NEAR + 1, owners, 2)
    far = refs[: len(odds)]
    refs = refs[len(odds) :]
    held = -(-blocks // owners)
    shards = refs[:held]
    counts, base, low_in, grad_in, down, up, bias, cot = refs[held : 8 + held]
    front_out, low_out, grad_out = refs[8 + held : 11 + held]
    outs = refs[11 + held :]
    batch, width = base.shape
    pooled = base[...]
    for part in range(1, held):
        rows = counts[part * shards[part].shape[0] : (part + 1) * shards[part].shape[0], :]
        pooled += lax.dot_general(
            rows, shards[part][...], (((0,), (0,)), ((), ())), preferred_element_type=F32
        )
    front = pooled.astype(BF16)
    front_out[...] = front
    low, grad = add_up(front, 0, down, up, cot, low_in[...], grad_in[...])
    for k, ref in zip(odds, far):
        x = wide(ref, span[1], batch)
        low, grad = add_up(x, (1 + k * slots + span[0]) * width, down, up, cot, low, grad)
    low = low.astype(BF16)
    grad = grad.astype(BF16)
    low_out[...] = low
    grad_out[...] = grad
    for k, out in zip(range(NEAR, owners, 2), outs):
        begin = 1 + k * slots + grad_span[0]
        grads_to(out, begin, grad_span[1], low, grad, down, up, bias, cot)


def grads_kernel(span, masks, slots, low, grad, down, up, bias, cot, _, *outs):
    for k, out in zip(masks, outs):
        begin = 1 + k * slots + span[0]
        grads_to(out, begin, span[1], low[...], grad[...], down, up, bias, cot)


def crossed_kernel(spans, owners, slots, *refs):
    meta = refs[0]
    chunks = len(spans)
    near = refs[1 : 1 + NEAR]
    count = owners - NEAR
    far = [refs[1 + NEAR + c * count : 1 + NEAR + (c + 1) * count] for c in range(chunks)]
    front, low, up, bias, _, out, held = refs[1 + NEAR + chunks * count :]
    batch, width = front.shape

    def gated(xs, begin):
        span = slice(begin * width, (begin + len(xs)) * width)
        gate = jnp.dot(low[...], up[:, span], preferred_element_type=F32)
        for i, x in enumerate(xs):
            part = gate[:, i * width : (i + 1) * width] + bias[begin + i : begin + i + 1, :]
            x = x.astype(F32)
            xs[i] = (x * part + x).astype(BF16)
        return xs

    out[:, :width] = gated([front[...]], 0)[0]
    runs = [(ref, k, 0, slots) for k, ref in enumerate(near)]
    runs += [(ref, k, *spans[c]) for c in range(chunks) for k, ref in enumerate(far[c], NEAR)]
    for ref, k, first, steps in runs:
        xs = [ref[i * batch : (i + 1) * batch, :] for i in range(steps)]
        for i, value in enumerate(gated(xs, 1 + k * slots + first)):
            held[k * slots + first + i] = value
    for table in range(out.shape[1] // width - 1):
        out[:, (table + 1) * width : (table + 2) * width] = held[meta[1, table]]


def summed(lines, masks, slot, grads, pad, rows, first=0):
    batch = lines.shape[1]
    position = lax.broadcasted_iota(jnp.int32, (rows, batch), 0) + first
    picks = [
        jnp.where(position == lines[k * pad + slot : k * pad + slot + 1, :], 1.0, 0.0).astype(BF16)
        for k in masks
    ]
    return jnp.dot(
        jnp.concatenate(picks, axis=1), jnp.concatenate(grads, axis=0), preferred_element_type=F32
    )


def near_scatter_kernel(slots, pad, *refs):
    lines = refs[0]
    near, out = refs[1:-1], refs[-1]
    batch = lines.shape[1]
    for slot in range(slots):
        grads = [ref[slot * batch : (slot + 1) * batch, :] for ref in near]
        out[slot] = summed(lines, range(NEAR), slot, grads, pad, out.shape[1])


def far_scatter_kernel(span, owners, pad, *refs):
    lines, near = refs[:2]
    far = refs[2 : 2 + owners - NEAR]
    out, held, sems = refs[-3:]
    rows = out.shape[2]
    batch = lines.shape[1]
    copies = []
    for step in range(span[1]):
        slot = span[0] + step
        grads = [ref[step * batch : (step + 1) * batch, :] for ref in far]
        half = rows // 2
        for part in range(2):
            here = slice(part * half, (part + 1) * half)
            more = summed(lines, range(NEAR, owners), slot, grads, pad, half, part * half)
            held[step, here, :] = near[slot, here, :] + more
            copies.append(
                pltpu.make_async_copy(
                    held.at[step, here], out.at[0, slot, here], sems.at[2 * step + part]
                )
            )
            copies[-1].start()
    for copy in copies:
        copy.wait()


def on_device(
    hot_slab,
    hot_ids,
    dense,
    cold_ids,
    table_slot,
    cold_tables,
    down_rank,
    up_rank,
    cross_bias,
    cotangent,
):
    batch, width = dense.shape
    owners = lax.axis_size("table")
    blocks = lax.axis_size("blk")
    slots, table_rows = cold_tables.shape[:2]
    rank = down_rank.shape[1]
    height = hot_slab.shape[0]
    total = owners * slots
    pad = -(-slots // 8) * 8
    row_spans, grad_spans = cut(slots, ROW_PARTS), cut(slots, GRAD_PARTS)
    assert owners & (owners - 1) == 0 and owners > NEAR
    far_count = owners - NEAR

    def call(kernel, shapes, operands, specs=None, *, mib, scratch=(), aliases=None, flops=4e9):
        return pl.pallas_call(
            kernel,
            out_shape=shapes,
            in_specs=[VMEM] * len(operands) if specs is None else specs,
            out_specs=[VMEM] * len(shapes),
            scratch_shapes=list(scratch),
            input_output_aliases=aliases or {},
            compiler_params=pltpu.CompilerParams(vmem_limit_bytes=mib << 20),
            cost_estimate=pl.CostEstimate(flops=int(flops), transcendentals=0, bytes_accessed=1 << 20),
        )(*operands)

    def swap(array, k):
        return lax.ppermute(array, "table", [(i, i ^ k) for i in range(owners)])

    def far_swap(arrays):
        return [swap(array, k) for k, array in enumerate(arrays, NEAR)]

    def shape(*dims, dtype=BF16):
        return jax.ShapeDtypeStruct(dims, dtype)

    ids = cold_ids.T
    far_ids = far_swap([ids] * far_count)
    near_ids = swap(ids, 1)
    shard = lax.ppermute(
        hot_slab,
        ("blk", "table"),
        [
            (peer(b, t, blocks) * owners + t, b * owners + t)
            for b in range(blocks)
            for t in range(owners)
        ],
    )
    (cover,) = call(cover_kernel, [shape(8, 128, dtype=jnp.int32)], [], mib=1)
    tables = cold_tables
    lines, meta, *sends = call(
        functools.partial(far_first_kernel, row_spans[0], owners, slots, pad),
        [shape(owners * pad, batch, dtype=jnp.int32), shape(8, 128, dtype=jnp.int32)]
        + [shape(row_spans[0][1] * batch + height, width)] * far_count,
        [table_slot, cover, ids, near_ids, *far_ids, tables],
        [SMEM] + [VMEM] * (owners + 2),
        scratch=[pltpu.SMEM((slots + 1,), jnp.int32)],
        mib=4,
        flops=1e9,
    )
    sends = call(
        tail_kernel,
        [shape(*array.shape) for array in sends],
        [shard, *sends],
        aliases={1 + i: i for i in range(far_count)},
        mib=1,
        flops=1e8,
    )
    far = [far_swap(sends)]
    again, *sends = call(
        functools.partial(far_kernel, row_spans[1], owners, pad),
        [shape(8, batch, dtype=jnp.int32)] + [shape(row_spans[1][1] * batch, width)] * far_count,
        [lines, tables],
        mib=4,
        flops=5e8,
    )
    far.append(far_swap(sends))
    features = (total + 1) * width
    (partner,) = call(
        functools.partial(partner_kernel, slots, pad),
        [shape(slots * batch + height, width)],
        [lines, again, tables, shard],
        mib=4,
        flops=5e8,
    )
    mine, down, up, cot, bias = call(
        functools.partial(near_kernel, owners, slots, pad),
        [
            shape(slots * batch, width),
            shape(features, rank),
            shape(rank, features),
            shape(batch, features),
            shape(-(-(total + 1) // 8) * 8, width, dtype=F32),
        ],
        [meta, lines, partner, tables]
        + [down_rank, up_rank, cotangent, cross_bias.reshape(-1, width)],
        [SMEM] + [VMEM] * 7,
        mib=6,
    )
    hot_rows = hot_ids.T
    near = [mine, swap(partner, 1)]

    (group,) = call(
        functools.partial(shards_kernel, owners),
        [shape(owners * height, width)],
        [shard, near[1], *far[0]],
        mib=1,
    )
    shards = [group]
    for mask in range(owners, blocks, owners):
        pairs = [(peer(b, mask, blocks), b) for b in range(blocks)]
        shards.append(lax.ppermute(group, "blk", pairs))

    counts, base = call(
        functools.partial(counts_kernel, owners, blocks),
        [
            shape(-(-blocks // owners) * owners * height, batch),
            shape(batch, width, dtype=F32),
        ],
        [group, hot_rows, dense],
        mib=2,
    )
    sums = [shape(batch, rank, dtype=F32)] * 2
    low, grad = call(
        functools.partial(sums_kernel, (0, slots), range(NEAR), slots),
        sums,
        [*near, down, up, cot],
        mib=6,
    )
    low, grad = call(
        functools.partial(sums_kernel, row_spans[0], range(NEAR, owners), slots),
        sums,
        [*far[0], down, up, cot, low, grad],
        mib=6,
    )
    low, grad = call(
        functools.partial(sums_kernel, row_spans[1], range(NEAR, owners, 2), slots),
        sums,
        [*far[1][::2], down, up, cot, low, grad],
        mib=6,
    )
    front, low, grad, *sends = call(
        functools.partial(second_kernel, row_spans[1], grad_spans[0], owners, slots, blocks),
        [shape(batch, width), shape(batch, rank), shape(batch, rank)]
        + [shape(grad_spans[0][1] * batch, width)] * (far_count // 2),
        [*far[1][1::2], *shards, counts, base, low, grad, down, up, bias, cot],
        mib=6,
    )
    odds = call(
        functools.partial(grads_kernel, grad_spans[0], range(NEAR + 1, owners, 2), slots),
        [shape(grad_spans[0][1] * batch, width)] * (far_count // 2),
        [low, grad, down, up, bias, cot, front],
        mib=6,
    )
    sends = [array for pair in zip(sends, odds) for array in pair]
    far_grads = [far_swap(sends)]
    sends = call(
        functools.partial(grads_kernel, grad_spans[1], range(NEAR, owners), slots),
        [shape(grad_spans[1][1] * batch, width)] * far_count,
        [low, grad, down, up, bias, cot, front],
        mib=6,
    )
    far_grads.append(far_swap(sends))
    near_grads = call(
        functools.partial(grads_kernel, (0, slots), range(NEAR), slots),
        [shape(slots * batch, width)] * NEAR,
        [low, grad, down, up, bias, cot, sends[0]],
        mib=6,
    )
    last_near = near_grads[0]
    near_grads = [near_grads[0], swap(near_grads[1], 1)]
    (crossed,) = call(
        functools.partial(crossed_kernel, row_spans, owners, slots),
        [shape(*cotangent.shape)],
        [meta, *near, *far[0], *far[1], front, low, up, bias, last_near],
        [SMEM] + [VMEM] * (NEAR + 2 * far_count + 5),
        scratch=[pltpu.VMEM((total, batch, width), BF16)],
        mib=6,
    )

    (near_sums,) = call(
        functools.partial(near_scatter_kernel, slots, pad),
        [shape(slots, table_rows, width, dtype=F32)],
        [lines, *near_grads],
        mib=6,
    )
    table_grad = []
    for chunk, (first, count) in enumerate(grad_spans):
        table_grad = [
            pl.pallas_call(
                functools.partial(far_scatter_kernel, (first, count), owners, pad),
                out_shape=shape(1, slots, table_rows, width, dtype=F32),
                in_specs=[VMEM] * (2 + far_count)
                + [pl.BlockSpec(memory_space=pl.ANY)] * len(table_grad),
                out_specs=pl.BlockSpec(memory_space=pl.ANY),
                scratch_shapes=[
                    pltpu.VMEM((count, table_rows, width), F32),
                    pltpu.SemaphoreType.DMA((2 * count,)),
                ],
                input_output_aliases={2 + far_count: 0} if table_grad else {},
                compiler_params=pltpu.CompilerParams(vmem_limit_bytes=6 << 20),
            )(lines, near_sums, *far_grads[chunk], *table_grad)
        ]
    (table_grad,) = table_grad
    return crossed, table_grad


def solution(mesh):
    placed = (
        P("blk", None),
        P(("blk", "table"), None),
        P(("blk", "table"), None),
        P(("blk", "table"), None),
        P(),
        P("table", None, None),
        P(),
        P(),
        P(),
        P(("blk", "table"), None),
    )

    return jax.shard_map(
        on_device,
        mesh=mesh,
        in_specs=placed,
        out_specs=(P(("blk", "table"), None), P("blk", "table", None, None)),
        check_vma=False,
    )
```
